512 devices in a mesh: dp: 16 (over y, z_hi), seq: 32 (over z_lo, x, core).
Axes of the slice: x: 4, y: 4, z: 16 (z_hi: 4, z_lo: 4; z = z_hi * 4 + z_lo), core: 2. Of those that a mesh axis runs over, the one named last changes fastest.
Arguments:
- tokens: bfloat16 [1024, 64, 1152], P(('dp', 'seq')), may hold values from -6 to 6
- spatial_qkv: bfloat16 [1024, 64, 1728], P(('dp', 'seq')), may hold values from -6 to 6
- wo_spatial: bfloat16 [576, 1152], replicated, may hold values from -0.25 to 0.25
- w_temporal: bfloat16 [1152, 1728], P(None, 'dp'), may hold values from -0.1875 to 0.1875
- wo_temporal: bfloat16 [576, 1152], replicated, may hold values from -0.25 to 0.25
- cotangent: bfloat16 [1024, 64, 1152], P(('dp', 'seq')), may hold values from -24 to 24
Outputs:
- block_out: bfloat16 [1024, 64, 1152], P(('dp', 'seq'))
- tokens_grad: bfloat16 [1024, 64, 1152], P(('dp', 'seq'))
- spatial_qkv_grad: bfloat16 [1024, 64, 1728], P(('dp', 'seq'))
- wo_spatial_grad: float32 [576, 1152], P('seq', 'dp')
- wo_temporal_grad: float32 [576, 1152], P('seq', 'dp')
The draws below stay inside these ranges and needn't reach their ends.
All inputs are finite; a program needn't handle non-finite values.
Results may differ from the reference program's by a relative error of at most 0.038.
Values may be sent and summed in bfloat16 or wider, within the bound.
A program may use at most 64 MiB of HBM per device.

```python
import math
import jax
import jax.numpy as jnp
from jax import lax

D = 1152
HEADS = 8
DH = 72
FRAMES = 16
FR_DEV = 2
PATCH = 64
HD = 576
NFR = 1024


def draw_spatial_qkv(key, part):
    keys = jax.random.split(jax.random.fold_in(key, 17), 7)
    base_shape = (NFR, PATCH, 3, HEADS, DH)
    base = jnp.clip(jax.random.normal(keys[0], base_shape, jnp.float32), -6.0, 6.0)
    signs = jnp.where(jax.random.bernoulli(keys[1], 0.5, (NFR, HEADS, DH)), 1.0, -1.0).astype(jnp.float32)
    strength = jax.random.uniform(keys[2], (NFR, HEADS), jnp.float32, 2.5, 6.0)
    margin = jax.random.uniform(keys[3], (NFR, HEADS), jnp.float32, 1.0, 3.0)
    query_pos = jax.random.randint(keys[4], (NFR, HEADS), 0, PATCH)
    first_pos = jax.random.randint(keys[5], (NFR, HEADS), 0, PATCH)
    second_pos = (first_pos + jax.random.randint(keys[6], (NFR, HEADS), 1, PATCH)) % PATCH
    patch_index = jnp.arange(PATCH).reshape(1, PATCH, 1)
    query_sel = (patch_index == query_pos[:, None, :])[..., None]
    first_sel = (patch_index == first_pos[:, None, :])[..., None]
    second_sel = (patch_index == second_pos[:, None, :])[..., None]
    column = jnp.arange(DH).reshape(1, 1, DH)
    reduction = margin * DH ** 0.5 / (4.0 * strength)
    lowered = jnp.where(column < 4, reduction[..., None], 0.0)
    query_plant = (strength[..., None] * signs)[:, None]
    first_plant = (6.0 * signs)[:, None]
    second_plant = ((6.0 - lowered) * signs)[:, None]
    query_part = jnp.where(query_sel, query_plant, base[:, :, 0])
    key_part = jnp.where(first_sel, first_plant, jnp.where(second_sel, second_plant, base[:, :, 1]))
    stacked = jnp.stack([query_part, key_part, base[:, :, 2]], axis=2)
    return stacked.reshape(NFR, PATCH, 3 * HEADS * DH).astype(jnp.bfloat16)


def strengthened(drawn, rng, source, target, shards_of, factor):
    def block_of(axis_at):
        return (jnp.arange(drawn.shape[axis_at]) // (drawn.shape[axis_at] // shards_of)).reshape((-1,) + (1,) * (drawn.ndim - 1 - axis_at))

    near = jax.random.permutation(rng, shards_of)[block_of(target)]
    far = (block_of(target) + shards_of // 2) % shards_of
    return jnp.where((block_of(source) == near) | (block_of(source) == far), factor * drawn, drawn)


def block_scale(own_key, dims, cuts, least, top_value):
    def one(dim, shards_of):
        steps = jax.random.uniform(jax.random.fold_in(jax.random.fold_in(own_key, 6), dim), (shards_of,), jnp.float32, least / len(cuts), top_value / len(cuts))
        return jnp.repeat(jnp.exp(steps), dims[dim] // shards_of).reshape((-1,) + (1,) * (len(dims) - dim - 1))

    factor_of = one(*cuts[0])
    for cut in cuts[1:]:
        factor_of = factor_of * one(*cut)
    return factor_of


def normal_values(key, extent, scale, reach, pieces=(), held_as=jnp.bfloat16):
    entries = jax.random.normal(key, extent, jnp.float32) * scale
    if len(pieces) > 0:
        entries = block_scale(key, extent, pieces, -0.22, 0.18) * entries
    return jnp.clip(entries, min=-reach, max=reach).astype(held_as)


def gaussian_with(stream_key, shape, scale, reach, cuts, heavy, kind=jnp.bfloat16):
    entries = scale * jax.random.normal(stream_key, shape, jnp.float32)
    if cuts:
        entries = entries * block_scale(stream_key, shape, cuts, -0.22, 0.18)
    return jnp.clip(strengthened(entries, jax.random.fold_in(stream_key, 3), *heavy), -reach, reach).astype(kind)


def setup_inputs(seed: int = 0) -> dict:
    seeds = jax.random.split(jax.random.key(seed), 7)
    tokens = normal_values(seeds[0], (NFR, PATCH, D), 1.0, 6.0, ((0, 512),))
    spatial_qkv = draw_spatial_qkv(jax.random.fold_in(seeds[6], 71), 0)
    wo_spatial = normal_values(seeds[2], (HD, D), HD ** -0.5, 0.25)
    w_temporal = normal_values(seeds[3], (D, 3 * HD), D ** -0.5, 0.1875, ((1, 16),))
    wo_temporal = normal_values(seeds[4], (HD, D), HD ** -0.5, 0.25)
    cotangent = gaussian_with(seeds[5], (NFR, PATCH, D), 1.0, 24.0, ((0, 512),), (0, 2, 128, 5.5))
    return dict(tokens=tokens, spatial_qkv=spatial_qkv, wo_spatial=wo_spatial, w_temporal=w_temporal, wo_temporal=wo_temporal, cotangent=cotangent)


def split_three(packed):
    inner_width = packed.shape[-1] // 3
    return (packed[..., :inner_width], packed[..., inner_width:2 * inner_width], packed[..., 2 * inner_width:])

def head_view(matrix):
    batch_size, length, inner_width = matrix.shape
    return matrix.astype(jnp.float32).reshape(batch_size, length, inner_width // DH, DH)

def attention_weights_of(query_heads, key_heads):
    scores = jnp.einsum('blhd,bmhd->bhlm', query_heads, key_heads) * (1.0 / math.sqrt(DH))
    return jax.nn.softmax(scores, axis=-1)

def attention(queries, key_rows, values):
    batch_size, length, inner_width = queries.shape
    weights_full = attention_weights_of(head_view(queries), head_view(key_rows))
    rounded = lax.optimization_barrier(weights_full.astype(jnp.bfloat16)).astype(jnp.float32)
    output = jnp.einsum('bhlm,bmhd->blhd', rounded, head_view(values))
    return output.reshape(batch_size, length, inner_width).astype(jnp.bfloat16)

def attention_grad(queries, key_rows, values, output_grad):
    batch_size, length, inner_width = queries.shape
    query_heads = head_view(queries)
    key_heads = head_view(key_rows)
    value_heads = head_view(values)
    grad_heads = head_view(output_grad)
    weights_full = attention_weights_of(query_heads, key_heads)
    rounded = lax.optimization_barrier(weights_full.astype(jnp.bfloat16)).astype(jnp.float32)
    value_grad = jnp.einsum('bhlm,blhd->bmhd', rounded, grad_heads)
    weight_grad = jnp.einsum('blhd,bmhd->bhlm', grad_heads, value_heads)
    centered = weight_grad - lax.optimization_barrier(jnp.sum(weights_full * weight_grad, axis=-1, keepdims=True))
    score_grad = (weights_full * centered * (1.0 / math.sqrt(DH))).astype(jnp.bfloat16)
    score_grad = lax.optimization_barrier(score_grad).astype(jnp.float32)
    query_grad = jnp.einsum('bhlm,bmhd->blhd', score_grad, key_heads)
    key_grad = jnp.einsum('bhlm,blhd->bmhd', score_grad, query_heads)
    joined = [part_grad.reshape(batch_size, length, inner_width) for part_grad in (query_grad, key_grad, value_grad)]
    return jnp.concatenate(joined, axis=-1).astype(jnp.bfloat16)

def to_clips(matrix, clip_count):
    frame_total, patch_share, channels = matrix.shape
    grouped = matrix.reshape(clip_count, FRAMES, patch_share, channels).transpose(0, 2, 1, 3)
    return grouped.reshape(clip_count * patch_share, FRAMES, channels)

def from_clips(matrix, clip_count):
    batch_rows, frame_count, channels = matrix.shape
    patch_share = batch_rows // clip_count
    grouped = matrix.reshape(clip_count, patch_share, frame_count, channels).transpose(0, 2, 1, 3)
    return grouped.reshape(clip_count * frame_count, patch_share, channels)

def group_sum(left, right):
    group_count = NFR // FR_DEV
    left_groups = left.reshape(group_count, FR_DEV * PATCH, left.shape[-1])
    right_groups = right.reshape(group_count, FR_DEV * PATCH, right.shape[-1])

    def add_group(running, pair):
        left_part, right_part = pair
        partial_value = jnp.dot(left_part.T, right_part, preferred_element_type=jnp.float32).astype(jnp.bfloat16)
        return (running + lax.optimization_barrier(partial_value).astype(jnp.float32), None)
    initial = jnp.zeros((left.shape[-1], right.shape[-1]), jnp.float32)
    total_sum, unused = lax.scan(add_group, initial, (left_groups, right_groups))
    return total_sum

def reference(tokens, spatial_qkv, wo_spatial, w_temporal, wo_temporal, cotangent):
    row_total = NFR * PATCH
    clip_count = NFR // FRAMES
    spatial_query, spatial_keys, spatial_values = split_three(spatial_qkv)
    spatial_out = attention(spatial_query, spatial_keys, spatial_values)
    spatial_rows = spatial_out.reshape(row_total, -1)
    hidden_rows = (tokens.reshape(row_total, D).astype(jnp.float32) + jnp.dot(spatial_rows, wo_spatial, preferred_element_type=jnp.float32)).astype(jnp.bfloat16)
    temporal_qkv = jnp.dot(hidden_rows, w_temporal, preferred_element_type=jnp.float32).astype(jnp.bfloat16)
    clip_qkv = to_clips(temporal_qkv.reshape(NFR, PATCH, -1), clip_count)
    temporal_query, temporal_keys, temporal_values = split_three(clip_qkv)
    temporal_out = from_clips(attention(temporal_query, temporal_keys, temporal_values), clip_count)
    temporal_rows = temporal_out.reshape(row_total, -1)
    block_out = (hidden_rows.astype(jnp.float32) + jnp.dot(temporal_rows, wo_temporal, preferred_element_type=jnp.float32)).astype(jnp.bfloat16)
    grad_rows = cotangent.reshape(row_total, D)
    out_grad = jnp.dot(grad_rows, wo_temporal.T, preferred_element_type=jnp.float32).astype(jnp.bfloat16)
    clip_grad = to_clips(out_grad.reshape(NFR, PATCH, -1), clip_count)
    temporal_qkv_grad = from_clips(attention_grad(temporal_query, temporal_keys, temporal_values, clip_grad), clip_count)
    projection_grad = jnp.dot(temporal_qkv_grad.reshape(row_total, -1), w_temporal.T, preferred_element_type=jnp.float32).astype(jnp.bfloat16)
    projection_grad = lax.optimization_barrier(projection_grad)
    tokens_grad = (grad_rows.astype(jnp.float32) + projection_grad.astype(jnp.float32)).astype(jnp.bfloat16)
    spatial_out_grad = jnp.dot(tokens_grad, wo_spatial.T, preferred_element_type=jnp.float32).astype(jnp.bfloat16)
    spatial_qkv_grad = attention_grad(spatial_query, spatial_keys, spatial_values, spatial_out_grad.reshape(NFR, PATCH, -1))
    wo_spatial_grad = group_sum(spatial_rows, tokens_grad)
    wo_temporal_grad = group_sum(temporal_rows, grad_rows)
    return (block_out.reshape(NFR, PATCH, D), tokens_grad.reshape(NFR, PATCH, D), spatial_qkv_grad, wo_spatial_grad, wo_temporal_grad)
```

```python
import functools
import math

import jax
import jax.numpy as jnp
from jax import lax
from jax.experimental import pallas as pl
from jax.experimental.pallas import tpu as pltpu
from jax.sharding import PartitionSpec as P

DH = 72
FRAMES = 16
MESH = pl.DeviceIdType.MESH
VMEM_LIMIT = 60 * 1024 * 1024


def coords():
    dp, seq = lax.axis_index("dp"), lax.axis_index("seq")
    return dp // 4, dp % 4, seq // 8, (seq // 2) % 4, seq % 2


def device(y, zh, zl, x, core):
    return (y * 4 + zh, (zl * 4 + x) * 2 + core)


def greet(partners):
    barrier = pltpu.get_barrier_semaphore()
    for partner in partners:
        pl.semaphore_signal(barrier, inc=1, device_id=partner, device_id_type=MESH)
    pl.semaphore_wait(barrier, len(partners))


def remote(src, dst, send_sem, recv_sem, target):
    return pltpu.make_async_remote_copy(
        src_ref=src, dst_ref=dst, send_sem=send_sem, recv_sem=recv_sem,
        device_id=target, device_id_type=MESH,
    )


def gather_kernel(w_ref, out_ref, own_sem, zs, zr, fs, fr, ss, sr, ps, pr):
    y, zh, zl, x, c = coords()
    rows = w_ref.shape[0] // 8
    u = (1 - c) * y + c * x
    v = (1 - c) * x + c * y

    def at(u_, v_):
        y_ = (1 - c) * u_ + c * v_
        x_ = (1 - c) * v_ + c * u_
        return device(y_, zh, zl, x_, c)

    firsts = [at((u + d) % 4, v) for d in range(1, 4)]
    seconds = [at(u, (v + d) % 4) for d in range(1, 4)]
    zs_to = [device(y, (zh + d) % 4, zl, x, c) for d in range(1, 4)]
    partner = device(y, zh, zl, x, 1 - c)
    greet(firsts + seconds + zs_to + [partner])

    piece = w_ref.at[pl.ds((c * 4 + x) * rows, rows)]
    mine = out_ref.at[zh, c, v, u]
    own = pltpu.make_async_copy(piece, mine, own_sem)
    own.start()
    pending = []

    def send(copy):
        copy.start()
        pending.append(copy)

    zcopies = {}
    for d in (1, 3, 2):
        zcopies[d] = remote(piece, mine, zs.at[d - 1], zr.at[d - 1], zs_to[d - 1])
        send(zcopies[d])
    own.wait()
    order = (0, 1, 3, 2)
    first, second, cross = {}, {}, {}
    for step in range(6):
        if step < 4:
            e = order[step]
            zset = (zh + 4 - e) % 4
            if e:
                zcopies[e].wait_recv()
            for d in range(1, 4):
                ref = out_ref.at[zset, c, v, u]
                first[e, d] = remote(ref, ref, fs.at[e, d - 1], fr.at[e, d - 1], firsts[d - 1])
                send(first[e, d])
        if 1 <= step < 5:
            e = order[step - 1]
            zset = (zh + 4 - e) % 4
            for d in range(1, 4):
                first[e, d].wait_recv()
            ref = out_ref.at[zset, c, v]
            for d in range(1, 4):
                second[e, d] = remote(ref, ref, ss.at[e, d - 1], sr.at[e, d - 1], seconds[d - 1])
                send(second[e, d])
            cross[e, 0] = remote(ref, ref, ps.at[e, 0], pr.at[e, 0], partner)
            send(cross[e, 0])
        if step >= 2:
            e = order[step - 2]
            zset = (zh + 4 - e) % 4
            for d in range(1, 4):
                second[e, d].wait_recv()
                ref = out_ref.at[zset, c, (v + 4 - d) % 4]
                cross[e, d] = remote(ref, ref, ps.at[e, d], pr.at[e, d], partner)
                send(cross[e, d])
    for e in range(4):
        for d in range(4):
            cross[e, d].wait_recv()
    for copy in pending:
        copy.wait_send()


def gather_weights(w_shard):
    depth = w_shard.shape[0]
    padded = jnp.pad(w_shard, ((0, 0), (0, 128 - w_shard.shape[1])))
    sems = pltpu.SemaphoreType.DMA
    gathered = pl.pallas_call(
        gather_kernel,
        out_shape=jax.ShapeDtypeStruct((4, 2, 4, 4, depth // 8, 128), jnp.bfloat16),
        in_specs=[pl.BlockSpec(memory_space=pltpu.VMEM)],
        out_specs=pl.BlockSpec(memory_space=pltpu.VMEM),
        scratch_shapes=[
            sems, sems((3,)), sems((3,)), sems((4, 3)), sems((4, 3)), sems((4, 3)), sems((4, 3)),
            sems((4, 4)), sems((4, 4)),
        ],
        compiler_params=pltpu.CompilerParams(
            collective_id=0, has_side_effects=True, vmem_limit_bytes=VMEM_LIMIT
        ),
        name="gather_weights",
    )(padded)
    return gathered


def whole_weights(gathered, width):
    zh, _, _, _, rows, lanes = gathered.shape
    upper = gathered[:, 0].transpose(1, 3, 2, 0, 4)
    lower = gathered[:, 1].transpose(2, 3, 1, 0, 4)
    both = jnp.stack([upper, lower])[..., :width]
    return both.reshape(8 * rows, 16 * width)


def exchange_kernel(count, *refs):
    srcs, dsts = refs[:count], refs[count : 2 * count]
    own_sem, send_sems, recv_sems = refs[2 * count :]
    y, zh, zl, x, c = coords()
    me = x * 2 + c
    others = [(me + d) % 8 for d in range(1, 8)]
    ids = [device(y, zh, zl, j // 2, j % 2) for j in others]
    greet(ids)
    copies = []
    for k in range(count):
        for n, d in enumerate((1, 7, 2, 6, 3, 5, 4)):
            copies.append(
                remote(
                    srcs[k].at[others[d - 1]], dsts[k].at[me], send_sems.at[k, d - 1],
                    recv_sems.at[k, d - 1], ids[d - 1],
                )
            )
            copies[-1].start()
    for k in range(count):
        own = pltpu.make_async_copy(srcs[k].at[me], dsts[k].at[me], own_sem)
        own.start()
        own.wait()
    for copy in copies:
        copy.wait()


def exchange(collective_id, *arrays):
    count = len(arrays)
    vmem = pl.BlockSpec(memory_space=pltpu.VMEM)
    sems = pltpu.SemaphoreType.DMA
    return pl.pallas_call(
        functools.partial(exchange_kernel, count),
        out_shape=[jax.ShapeDtypeStruct(a.shape, a.dtype) for a in arrays],
        in_specs=[vmem] * count,
        out_specs=[vmem] * count,
        scratch_shapes=[sems, sems((count, 7)), sems((count, 7))],
        compiler_params=pltpu.CompilerParams(
            collective_id=collective_id, has_side_effects=True, vmem_limit_bytes=VMEM_LIMIT
        ),
        name=f"exchange_{collective_id}",
    )(*arrays)


def sum_kernel(
    lt_ref, r_ref, out_ref, ltx, rx, xs, xr, ysend, yrecv, zsend, zrecv,
    os_, or_, xss, xrs, yss, yrs, zss, zrs,
):
    y, zh, zl, x, c = coords()
    weights = lt_ref.shape[0]
    partner = device(y, zh, zl, x, 1 - c)
    xs_to = [device(y, zh, zl, (x + d) % 4, c) for d in range(1, 4)]
    ys_to = [device((y + d) % 4, zh, zl, x, c) for d in range(1, 4)]
    zpos = zh * 4 + zl
    z_at = [(zpos + d) % 16 for d in range(1, 16)]
    zs_to = [device(y, z // 4, z % 4, x, c) for z in z_at]
    greet([partner] + xs_to + ys_to + zs_to)
    swaps = []
    for w in range(weights):
        pair = (
            remote(lt_ref.at[w, 1 - c], ltx.at[w], os_.at[w, 0], or_.at[w, 0], partner),
            remote(r_ref.at[w], rx.at[w], os_.at[w, 1], or_.at[w, 1], partner),
        )
        for copy in pair:
            copy.start()
        swaps.append(pair)
    done = []
    xcopies = []
    for w in range(weights):
        for copy in swaps[w]:
            copy.wait()
        left, right = lt_ref[w, c], r_ref[w]
        for k in range(4):
            rows = slice(k * 80, (k + 1) * 80)
            total = jnp.dot(left[rows], right, preferred_element_type=jnp.float32) + jnp.dot(
                ltx[w, rows], rx[w], preferred_element_type=jnp.float32
            )
            xs[w, k] = total.astype(jnp.bfloat16)
        row = []
        for d in (1, 3, 2):
            row.append(
                remote(xs.at[w, (x + d) % 4], xr.at[w, d - 1], xss.at[w, d - 1], xrs.at[w, d - 1], xs_to[d - 1])
            )
            row[-1].start()
        xcopies.append(row)
    ycopies = []
    for w in range(weights):
        for copy in xcopies[w]:
            copy.wait()
        total = xs[w, x].astype(jnp.float32)
        for d in range(3):
            total += xr[w, d].astype(jnp.float32)
        for k in range(4):
            ysend[w, k, :, 0:288] = total[:, k * 288 : (k + 1) * 288].astype(jnp.bfloat16)
        row = []
        for d in (1, 3, 2):
            row.append(
                remote(ysend.at[w, (y + d) % 4], yrecv.at[w, d - 1], yss.at[w, d - 1], yrs.at[w, d - 1], ys_to[d - 1])
            )
            row[-1].start()
        ycopies.append(row)
    zcopies = []
    for w in range(weights):
        for copy in ycopies[w]:
            copy.wait()
        total = ysend[w, y].astype(jnp.float32)
        for d in range(3):
            total += yrecv[w, d].astype(jnp.float32)
        for zh_ in range(4):
            for zl_ in range(4):
                zsend[w, zh_ * 4 + zl_, 0:18, 0:72] = total[
                    zl_ * 18 : (zl_ + 1) * 18, zh_ * 72 : (zh_ + 1) * 72
                ]
        row = []
        for d in range(1, 16):
            row.append(
                remote(
                    zsend.at[w, z_at[d - 1]], zrecv.at[w, d - 1], zss.at[w, d - 1], zrs.at[w, d - 1], zs_to[d - 1]
                )
            )
            row[-1].start()
        zcopies.append(row)
    for w in range(weights):
        total = zsend[w, zpos]
        for d in range(15):
            zcopies[w][d].wait()
            total += zrecv[w, d]
        out_ref[w] = total


def weight_sums(lefts, rights):
    weights, rows, inner = lefts.shape
    width = rights.shape[-1]
    by_core = lefts.reshape(weights, rows, 4, 4, 2, 18).transpose(0, 4, 3, 2, 5, 1)
    by_core = by_core.reshape(weights, 2, 4, 72, rows)
    by_core = jnp.pad(by_core, ((0, 0), (0, 0), (0, 0), (0, 8), (0, 0)))
    by_core = by_core.reshape(weights, 2, 320, rows)
    vmem = pl.BlockSpec(memory_space=pltpu.VMEM)
    sems = pltpu.SemaphoreType.DMA
    bf, f32 = jnp.bfloat16, jnp.float32
    out = pl.pallas_call(
        sum_kernel,
        out_shape=jax.ShapeDtypeStruct((weights, 24, 128), f32),
        in_specs=[vmem, vmem],
        out_specs=vmem,
        scratch_shapes=[
            pltpu.VMEM((weights, 320, rows), bf),
            pltpu.VMEM((weights, rows, width), bf),
            pltpu.VMEM((weights, 4, 80, width), bf),
            pltpu.VMEM((weights, 3, 80, width), bf),
            pltpu.VMEM((weights, 4, 80, 384), bf),
            pltpu.VMEM((weights, 3, 80, 384), bf),
            pltpu.VMEM((weights, 16, 24, 128), f32),
            pltpu.VMEM((weights, 15, 24, 128), f32),
            sems((weights, 2)), sems((weights, 2)),
            sems((weights, 3)), sems((weights, 3)),
            sems((weights, 3)), sems((weights, 3)),
            sems((weights, 15)), sems((weights, 15)),
        ],
        compiler_params=pltpu.CompilerParams(
            collective_id=9, has_side_effects=True, vmem_limit_bytes=VMEM_LIMIT
        ),
        name="weight_sums",
    )(by_core, rights)
    return out[:, :18, :72]


def split_three(packed):
    inner_width = packed.shape[-1] // 3
    return (
        packed[..., :inner_width],
        packed[..., inner_width : 2 * inner_width],
        packed[..., 2 * inner_width :],
    )


def head_view(matrix):
    batch_size, length, inner_width = matrix.shape
    return matrix.reshape(batch_size, length, inner_width // DH, DH)


def attention_weights_of(query_heads, key_heads):
    scores = jnp.einsum(
        "blhd,bmhd->bhlm", query_heads, key_heads, preferred_element_type=jnp.float32
    ) * (1.0 / math.sqrt(DH))
    return jax.nn.softmax(scores, axis=-1)


def attention(queries, key_rows, values):
    batch_size, length, inner_width = queries.shape
    weights_full = attention_weights_of(head_view(queries), head_view(key_rows))
    rounded = weights_full.astype(jnp.bfloat16)
    output = jnp.einsum(
        "bhlm,bmhd->blhd", rounded, head_view(values), preferred_element_type=jnp.float32
    )
    return output.reshape(batch_size, length, inner_width).astype(jnp.bfloat16)


def attention_grad(queries, key_rows, values, output_grad):
    batch_size, length, inner_width = queries.shape
    query_heads = head_view(queries)
    key_heads = head_view(key_rows)
    value_heads = head_view(values)
    grad_heads = head_view(output_grad)
    weights_full = attention_weights_of(query_heads, key_heads)
    rounded = weights_full.astype(jnp.bfloat16)
    value_grad = jnp.einsum(
        "bhlm,blhd->bmhd", rounded, grad_heads, preferred_element_type=jnp.float32
    )
    weight_grad = jnp.einsum(
        "blhd,bmhd->bhlm", grad_heads, value_heads, preferred_element_type=jnp.float32
    )
    centered = weight_grad - jnp.sum(weights_full * weight_grad, axis=-1, keepdims=True)
    score_grad = (weights_full * centered * (1.0 / math.sqrt(DH))).astype(jnp.bfloat16)
    query_grad = jnp.einsum(
        "bhlm,bmhd->blhd", score_grad, key_heads, preferred_element_type=jnp.float32
    )
    key_grad = jnp.einsum(
        "bhlm,blhd->bmhd", score_grad, query_heads, preferred_element_type=jnp.float32
    )
    joined = [
        part_grad.reshape(batch_size, length, inner_width)
        for part_grad in (query_grad, key_grad, value_grad)
    ]
    return jnp.concatenate(joined, axis=-1).astype(jnp.bfloat16)


def times_transposed(left, right):
    return lax.dot_general(
        left, right, (((1,), (1,)), ((), ())), preferred_element_type=jnp.float32
    )


def by_peer(matrix):
    frames, patches, width = matrix.shape
    return matrix.reshape(frames, 8, patches // 8, width).transpose(1, 0, 2, 3).reshape(8, -1, width)


def from_peer(blocks, frames):
    peers, rows, width = blocks.shape
    return (
        blocks.reshape(peers, frames, rows // frames, width)
        .transpose(1, 0, 2, 3)
        .reshape(frames * peers * rows // frames, width)
    )


def clip_rows(blocks, frames):
    peers, rows, width = blocks.shape
    return (
        blocks.reshape(peers, frames, rows // frames, width)
        .transpose(2, 0, 1, 3)
        .reshape(rows // frames, peers * frames, width)
    )


def peer_blocks(rows, frames):
    patches, total, width = rows.shape
    return (
        rows.reshape(patches, total // frames, frames, width)
        .transpose(1, 2, 0, 3)
        .reshape(total // frames, frames * patches, width)
    )


def shards(tokens, spatial_qkv, wo_spatial, w_temporal, wo_temporal, cotangent):
    frames_dev, patches, feature_width = tokens.shape
    row_total = frames_dev * patches
    width = w_temporal.shape[1]
    weights = whole_weights(gather_weights(w_temporal), width)
    spatial_query, spatial_keys, spatial_values = split_three(spatial_qkv)
    spatial_out = attention(spatial_query, spatial_keys, spatial_values)
    spatial_rows = spatial_out.reshape(row_total, -1)
    hidden_rows = (
        tokens.reshape(row_total, feature_width).astype(jnp.float32)
        + jnp.dot(spatial_rows, wo_spatial, preferred_element_type=jnp.float32)
    ).astype(jnp.bfloat16)
    grad_rows = cotangent.reshape(row_total, feature_width)
    out_grad = times_transposed(grad_rows, wo_temporal).astype(jnp.bfloat16)
    hidden_p, out_grad_p = exchange(
        1,
        by_peer(hidden_rows.reshape(frames_dev, patches, -1)),
        by_peer(out_grad.reshape(frames_dev, patches, -1)),
    )
    hidden_clip = clip_rows(hidden_p, frames_dev)
    qkv = jnp.dot(
        hidden_clip.reshape(row_total, -1), weights, preferred_element_type=jnp.float32
    ).astype(jnp.bfloat16)
    qkv = qkv.reshape(8, FRAMES, -1)
    temporal_query, temporal_keys, temporal_values = split_three(qkv)
    temporal_clip = attention(temporal_query, temporal_keys, temporal_values)
    qkv_grad = attention_grad(
        temporal_query, temporal_keys, temporal_values, clip_rows(out_grad_p, frames_dev)
    )
    projection_clip = times_transposed(qkv_grad.reshape(row_total, -1), weights).astype(jnp.bfloat16)
    projection_p, temporal_p = exchange(
        2,
        peer_blocks(projection_clip.reshape(8, FRAMES, -1), frames_dev),
        peer_blocks(temporal_clip, frames_dev),
    )
    projection_grad = from_peer(projection_p, frames_dev)
    temporal_rows = from_peer(temporal_p, frames_dev)
    block_out = (
        hidden_rows.astype(jnp.float32)
        + jnp.dot(temporal_rows, wo_temporal, preferred_element_type=jnp.float32)
    ).astype(jnp.bfloat16)
    tokens_grad = (grad_rows.astype(jnp.float32) + projection_grad.astype(jnp.float32)).astype(
        jnp.bfloat16
    )
    spatial_out_grad = (
        times_transposed(tokens_grad, wo_spatial)
        .astype(jnp.bfloat16)
        .reshape(frames_dev, patches, -1)
    )
    spatial_qkv_grad = attention_grad(spatial_query, spatial_keys, spatial_values, spatial_out_grad)
    sums = weight_sums(
        jnp.stack([spatial_rows, temporal_rows]), jnp.stack([tokens_grad, grad_rows])
    )
    return (
        block_out.reshape(frames_dev, patches, feature_width),
        tokens_grad.reshape(frames_dev, patches, feature_width),
        spatial_qkv_grad,
        sums[0],
        sums[1],
    )


def solution(mesh):
    placed = (
        P(("dp", "seq"), None, None),
        P(("dp", "seq"), None, None),
        P(),
        P(None, "dp"),
        P(),
        P(("dp", "seq"), None, None),
    )
    return jax.shard_map(
        shards,
        mesh=mesh,
        in_specs=placed,
        out_specs=(
            P(("dp", "seq"), None, None),
            P(("dp", "seq"), None, None),
            P(("dp", "seq"), None, None),
            P("seq", "dp"),
            P("seq", "dp"),
        ),
        check_vma=False,
    )
```

```python
import functools
import math

import jax
import jax.numpy as jnp
import numpy as np
from jax import lax
from jax.experimental import pallas as pl
from jax.experimental.pallas import tpu as pltpu
from jax.sharding import PartitionSpec as P

DH = 72
HEADS = 8
HD = 576
D = 1152
ROWS = 128
COLS = 108
SCALE = 1.0 / math.sqrt(DH)
MESH = pl.DeviceIdType.MESH
BF = jnp.bfloat16
F32 = jnp.float32


def device(y, zh, zl, x, core):
    return (y * 4 + zh, (zl * 4 + x) * 2 + core)


def nt(left, right):
    return lax.dot_general(left, right, (((1,), (1,)), ((), ())), preferred_element_type=F32)


def tn(left, right):
    return lax.dot_general(left, right, (((0,), (0,)), ((), ())), preferred_element_type=F32)


def nn(left, right):
    return jnp.dot(left, right, preferred_element_type=F32)


def head(ref, n):
    return ref[:, n * DH : (n + 1) * DH]


def attend(qkv_ref, mask, p_ref, out_ref, heads):
    for h in heads:
        scores = nt(head(qkv_ref, h), head(qkv_ref, HEADS + h)) * SCALE
        scores = jnp.where(mask, scores, -1e30)
        scores = jnp.exp(scores - jnp.max(scores, axis=-1, keepdims=True))
        weights = scores / jnp.sum(scores, axis=-1, keepdims=True)
        p_ref[h] = weights
        out = nn(weights.astype(BF), head(qkv_ref, 2 * HEADS + h))
        out_ref[:, h * DH : (h + 1) * DH] = out.astype(BF)


def attend_grad(qkv_ref, p_ref, g_ref, grad_ref, heads):
    for h in heads:
        weights = p_ref[h]
        grad = head(g_ref, h)
        value_grad = tn(weights.astype(BF), grad)
        weight_grad = nt(grad, head(qkv_ref, 2 * HEADS + h))
        centered = weight_grad - jnp.sum(weights * weight_grad, axis=-1, keepdims=True)
        score_grad = (weights * centered * SCALE).astype(BF)
        query_grad = nn(score_grad, head(qkv_ref, HEADS + h))
        key_grad = tn(score_grad, head(qkv_ref, h))
        for part, value in enumerate((query_grad, key_grad, value_grad)):
            at = (part * HEADS + h) * DH
            grad_ref[:, at : at + DH] = value.astype(BF)


def to_peers(value, send_ref):
    for j in range(8):
        block = jnp.concatenate([value[8 * j : 8 * j + 8], value[64 + 8 * j : 72 + 8 * j]], axis=0)
        send_ref[j] = block.astype(BF)


def from_peers(recv_ref):
    blocks = [recv_ref[j].astype(F32) for j in range(8)]
    return jnp.concatenate([b[:8] for b in blocks] + [b[8:] for b in blocks], axis=0)


def kernel(
    tokens_hbm, sqkv_hbm, wos_hbm, w_hbm, wot_hbm, cot_hbm, pick_hbm,
    block_hbm, tgrad_hbm, sgrad_hbm, sums_hbm,
    tok, sqkv, wos, wraw, wpad, wot, cot, pick, wbuf,
    hid, hid_s, hid_r, og_s, og_r, pg_s, pg_r, to_s, to_r,
    ps_ref, pt_ref, so, tqkv, tqkvp, to, og, dqkv, tgrad, sog, sgrad, block, trow,
    lt, ltx, rx, gsend, grecv, ysend, yrecv, zsend, zrecv, sums,
    load_sems, out_sems, own_sem,
    zss, zrs, fss, frs, sss, srs, css, crs, ass, ars, oss, ors, xss, xrs, yss, yrs, rss, rrs,
):
    dp, seq = lax.axis_index("dp"), lax.axis_index("seq")
    y, zh, zl, x, c = dp // 4, dp % 4, seq // 8, (seq // 2) % 4, seq % 2
    u = (1 - c) * y + c * x
    v = (1 - c) * x + c * y
    zpos = zh * 4 + zl

    def at(u_, v_):
        return device((1 - c) * u_ + c * v_, zh, zl, (1 - c) * v_ + c * u_, c)

    partner = device(y, zh, zl, x, 1 - c)
    me = x * 2 + c
    peers = [(me + d) % 8 for d in range(1, 8)]
    peer_ids = [device(y, zh, zl, j // 2, j % 2) for j in peers]
    y_ids = [device((y + d) % 4, zh, zl, x, c) for d in range(1, 4)]
    x_ids = [device(y, zh, zl, (x + d) % 4, c) for d in range(1, 4)]
    z_at = [(zpos + d) % 16 for d in range(1, 16)]
    z_ids = [device(y, z // 4, z % 4, x, c) for z in z_at]
    everyone = peer_ids + y_ids + z_ids

    barrier = pltpu.get_barrier_semaphore()
    for target in everyone:
        pl.semaphore_signal(barrier, inc=1, device_id=target, device_id_type=MESH)

    loads = {}
    for n, (name, src, dst) in enumerate(
        (
            ("w", w_hbm, wraw), ("sqkv", sqkv_hbm, sqkv), ("cot", cot_hbm, cot), ("wot", wot_hbm, wot),
            ("wos", wos_hbm, wos), ("tok", tokens_hbm, tok), ("pick", pick_hbm, pick),
        )
    ):
        loads[name] = pltpu.make_async_copy(src, dst, load_sems.at[n])
        loads[name].start()
    pending = []

    def send(src, dst, send_sem, recv_sem, target):
        copy = pltpu.make_async_remote_copy(
            src_ref=src, dst_ref=dst, send_sem=send_sem, recv_sem=recv_sem,
            device_id=target, device_id_type=MESH,
        )
        copy.start()
        pending.append(copy)
        return copy

    loads["w"].wait()
    wpad[...] = jnp.concatenate([wraw[...], jnp.zeros((D, 128 - COLS), BF)], axis=1)

    def ring(slot, low, high, pos, ids, ss, rs):
        state = {}

        def start():
            ref = slot(pos)
            state["up"] = send(ref, ref, ss.at[0], rs.at[0], ids[0])
            state["down"] = send(ref, ref, ss.at[1], rs.at[1], ids[2])

        def relay():
            state["up"].wait_recv()
            ref = low(slot((pos + 3) % 4))
            state["up2"] = send(ref, ref, ss.at[2], rs.at[2], ids[0])
            state["down"].wait_recv()
            ref = high(slot((pos + 1) % 4))
            state["down2"] = send(ref, ref, ss.at[3], rs.at[3], ids[2])

        def finish():
            state["up2"].wait_recv()
            state["down2"].wait_recv()

        return start, relay, finish

    def piece_low(ref):
        return ref.at[pl.ds(0, 80)]

    def piece_high(ref):
        return ref.at[pl.ds(80, 64)]

    zring_ids = [device(y, (zh + d) % 4, zl, x, c) for d in range(1, 4)]
    u_ids = [at((u + d) % 4, v) for d in range(1, 4)]
    v_ids = [at(u, (v + d) % 4) for d in range(1, 4)]
    zr = ring(lambda p: wbuf.at[p, c, v, u], piece_low, piece_high, zh, zring_ids, zss, zrs)
    order = (0, 1, 3, 2)
    zsets = [(zh + 4 - e) % 4 for e in order]
    fr = [
        ring(lambda p, s=s: wbuf.at[s, c, v, p], piece_low, piece_high, u, u_ids, fss.at[i], frs.at[i])
        for i, s in enumerate(zsets)
    ]
    sr = [
        ring(
            lambda p, s=s: wbuf.at[s, c, p], lambda r: r.at[pl.ds(0, 2)], lambda r: r.at[pl.ds(2, 2)],
            v, v_ids, sss.at[i], srs.at[i],
        )
        for i, s in enumerate(zsets)
    ]
    crosses = {}

    def cross(i, d):
        ref = wbuf.at[zsets[i], c, (v + d) % 4]
        crosses[i, d] = send(ref, ref, css.at[i, d], crs.at[i, d], partner)

    def stage_c(i):
        fr[i][2]()
        sr[i][0]()
        cross(i, 0)

    def stage_d(i):
        sr[i][1]()
        cross(i, 3)
        cross(i, 1)

    def stage_e(i):
        sr[i][2]()
        cross(i, 2)

    def stage_f(i):
        for d in range(4):
            crosses[i, d].wait_recv()

    def gather():
        own = pltpu.make_async_copy(wpad.at[pl.ds((c * 4 + x) * 144, 144)], wbuf.at[zh, c, v, u], own_sem)
        own.start()
        own.wait()
        zr[0]()
        fr[0][0]()
        yield
        fr[0][1]()
        yield
        zr[1]()
        fr[1][0]()
        fr[2][0]()
        stage_c(0)
        yield
        fr[1][1]()
        fr[2][1]()
        stage_d(0)
        yield
        zr[2]()
        fr[3][0]()
        stage_c(1)
        stage_c(2)
        stage_e(0)
        yield
        fr[3][1]()
        stage_d(1)
        stage_d(2)
        yield
        stage_f(0)
        yield
        stage_c(3)
        stage_e(1)
        stage_e(2)
        yield
        stage_f(1)
        yield
        stage_d(3)
        yield
        stage_f(2)
        yield
        stage_e(3)
        yield
        stage_f(3)
        yield

    def exchange(n, src, dst):
        copies = []
        for d in (1, 7, 2, 6, 3, 5, 4):
            copies.append(
                send(src.at[peers[d - 1]], dst.at[me], ass.at[n, d - 1], ars.at[n, d - 1], peer_ids[d - 1])
            )
        dst[me] = src[me]
        return copies

    def arrived(copies):
        for copy in copies:
            copy.wait_recv()

    def weight_sum(w, left_ref, right_ref):
        lt[w] = nt(pick[...], left_ref[...]).astype(BF).reshape(2, 320, ROWS)
        swap = (
            send(lt.at[w, 1 - c], ltx.at[w], oss.at[w, 0], ors.at[w, 0], partner),
            send(right_ref, rx.at[w], oss.at[w, 1], ors.at[w, 1], partner),
        )
        yield
        arrived(swap)
        for xk in range(4):
            rows = pl.ds(xk * 80, 80)
            total = nn(lt[w, c, rows], right_ref[...]) + nn(ltx[w, rows], rx[w])
            for yk in range(4):
                gsend[w, (1 - c) * xk + c * yk, (1 - c) * yk + c * xk, :, 0:288] = total[
                    :, yk * 288 : (yk + 1) * 288
                ].astype(BF)
        first_at = (1 - c) * x + c * y
        second_at = (1 - c) * y + c * x

        def step_id(first, d):
            dx = (1 - c) * d if first else c * d
            dy = d - dx
            return device((y + dy) % 4, zh, zl, (x + dx) % 4, c)

        copies = [
            send(
                gsend.at[w, (first_at + d) % 4], grecv.at[w, d - 1], xss.at[w, d - 1], xrs.at[w, d - 1],
                step_id(True, d),
            )
            for d in (1, 3, 2)
        ]
        yield
        arrived(copies)
        for k in range(4):
            total = gsend[w, first_at, k].astype(F32)
            for d in range(3):
                total += grecv[w, d, k].astype(F32)
            ysend[w, k] = total.astype(BF)
        copies = [
            send(
                ysend.at[w, (second_at + d) % 4], yrecv.at[w, d - 1], yss.at[w, d - 1], yrs.at[w, d - 1],
                step_id(False, d),
            )
            for d in (1, 3, 2)
        ]
        yield
        arrived(copies)
        total = ysend[w, second_at].astype(F32)
        for d in range(3):
            total += yrecv[w, d].astype(F32)
        for zh_ in range(4):
            for zl_ in range(4):
                zsend[w, zh_ * 4 + zl_, 0:18, 0:72] = total[
                    zl_ * 18 : (zl_ + 1) * 18, zh_ * 72 : (zh_ + 1) * 72
                ].astype(BF)
        copies = [
            send(
                zsend.at[w, z_at[d - 1]], zrecv.at[w, d - 1], rss.at[w, d - 1], rrs.at[w, d - 1], z_ids[d - 1]
            )
            for d in range(1, 16)
        ]
        yield
        arrived(copies)
        total = zsend[w, zpos].astype(F32)
        for d in range(15):
            total += zrecv[w, d].astype(F32)
        sums[w] = total
        yield

    row = lax.broadcasted_iota(jnp.int32, (ROWS, ROWS), 0)
    col = lax.broadcasted_iota(jnp.int32, (ROWS, ROWS), 1)
    same_frame = (row // 64) == (col // 64)
    same_patch = (row % 8) == (col % 8)

    loads["cot"].wait()
    loads["wot"].wait()
    to_peers(nt(cot[...], wot[...]), og_s)
    loads["sqkv"].wait()

    pl.semaphore_wait(barrier, len(everyone))
    steps = gather()
    next(steps)
    attend(sqkv, same_frame, ps_ref, so, range(0, 2))
    next(steps)
    attend(sqkv, same_frame, ps_ref, so, range(2, 5))
    next(steps)
    attend(sqkv, same_frame, ps_ref, so, range(5, 8))
    next(steps)
    loads["wos"].wait()
    loads["tok"].wait()
    loads["pick"].wait()
    hidden = tok[...].astype(F32) + nn(so[...], wos[...])
    hid[...] = hidden.astype(BF)
    to_peers(hidden, hid_s)
    hidden_copies = exchange(0, hid_s, hid_r)
    grad_copies = exchange(1, og_s, og_r)
    next(steps)
    next(steps)
    arrived(hidden_copies)

    def shard_of(s, y_):
        upper = wbuf[s, 0, :, y_].reshape(HD, 128)
        lower = wbuf[s, 1, y_].reshape(HD, 128)
        return jnp.concatenate([upper, lower], axis=0)

    def project(i):
        rows = hid_r[...].reshape(ROWS, D)
        for pair in range(2):
            both = jnp.concatenate([shard_of(zsets[i], 2 * pair), shard_of(zsets[i], 2 * pair + 1)], axis=1)
            out = nn(rows, both).astype(BF)
            for k in range(2):
                tqkvp[(2 * pair + k) * 4 + zsets[i]] = out[:, k * 128 : (k + 1) * 128]

    for i in range(4):
        next(steps)
        if i < 3:
            next(steps)
        project(i)
    for s in range(16):
        tqkv[:, s * COLS : (s + 1) * COLS] = tqkvp[s, :, 0:COLS]

    attend(tqkv, same_patch, pt_ref, to, range(8))
    to_s[...] = to[...].reshape(8, 16, HD)
    out_copies = exchange(2, to_s, to_r)
    arrived(grad_copies)
    og[...] = og_r[...].reshape(ROWS, HD)
    attend_grad(tqkv, pt_ref, og, dqkv, range(8))
    total = None
    for pair in range(8):
        grads, weights = [], []
        for k in range(2):
            s = 2 * pair + k
            grads += [dqkv[:, s * COLS : (s + 1) * COLS], jnp.zeros((ROWS, 128 - COLS), BF)]
            weights.append(shard_of(s % 4, s // 4))
        part = nt(jnp.concatenate(grads, axis=1), jnp.concatenate(weights, axis=1))
        total = part if total is None else total + part
    pg_s[...] = total.astype(BF).reshape(8, 16, D)
    projection_copies = exchange(3, pg_s, pg_r)

    arrived(out_copies)
    rows = from_peers(to_r).astype(BF)
    trow[...] = rows
    temporal_sum = weight_sum(1, trow, cot)
    next(temporal_sum)
    block[...] = (hid[...].astype(F32) + nn(rows, wot[...])).astype(BF)
    outs = [pltpu.make_async_copy(block, block_hbm, out_sems.at[0])]
    outs[0].start()
    next(temporal_sum)
    arrived(projection_copies)
    tgrad[...] = (cot[...].astype(F32) + from_peers(pg_r)).astype(BF)
    outs.append(pltpu.make_async_copy(tgrad, tgrad_hbm, out_sems.at[1]))
    outs[1].start()
    spatial_sum = weight_sum(0, so, tgrad)
    next(spatial_sum)
    sog[...] = nt(tgrad[...], wos[...]).astype(BF)
    next(spatial_sum)
    next(temporal_sum)
    attend_grad(sqkv, ps_ref, sog, sgrad, range(0, 4))
    next(temporal_sum)
    attend_grad(sqkv, ps_ref, sog, sgrad, range(4, 8))
    outs.append(pltpu.make_async_copy(sgrad, sgrad_hbm, out_sems.at[2]))
    outs[2].start()
    next(spatial_sum)
    next(spatial_sum)
    next(temporal_sum)
    next(spatial_sum)
    outs.append(pltpu.make_async_copy(sums, sums_hbm, out_sems.at[3]))
    outs[3].start()
    for copy in outs:
        copy.wait()
    for copy in pending:
        copy.wait_send()


def picker():
    pick = np.zeros((2, 4, 80, HD), np.float32)
    for zl in range(4):
        for x in range(4):
            for core in range(2):
                for i in range(18):
                    pick[core, x, zl * 18 + i, ((zl * 4 + x) * 2 + core) * 18 + i] = 1
    return jnp.asarray(pick.reshape(640, HD), BF)


def shards(tokens, spatial_qkv, wo_spatial, w_temporal, wo_temporal, cotangent):
    frames, patches, _ = tokens.shape
    sems = pltpu.SemaphoreType.DMA

    def vm(*shape, dtype=BF):
        return pltpu.VMEM(shape, dtype)

    scratch = [
        vm(ROWS, D), vm(ROWS, 3 * HD), vm(HD, D), vm(D, COLS), vm(D, 128), vm(HD, D), vm(ROWS, D),
        vm(640, HD), vm(4, 2, 4, 4, 144, 128),
        vm(ROWS, D), vm(8, 16, D), vm(8, 16, D), vm(8, 16, HD), vm(8, 16, HD),
        vm(8, 16, D), vm(8, 16, D), vm(8, 16, HD), vm(8, 16, HD),
        vm(8, ROWS, ROWS, dtype=F32), vm(8, ROWS, ROWS, dtype=F32),
        vm(ROWS, HD), vm(ROWS, 3 * HD), vm(16, ROWS, 128), vm(ROWS, HD), vm(ROWS, HD),
        vm(ROWS, 3 * HD), vm(ROWS, D), vm(ROWS, HD), vm(ROWS, 3 * HD), vm(ROWS, D), vm(ROWS, HD),
        vm(2, 2, 320, ROWS), vm(2, 320, ROWS), vm(2, ROWS, D),
        vm(2, 4, 4, 80, 384), vm(2, 3, 4, 80, 384), vm(2, 4, 80, 384), vm(2, 3, 80, 384),
        vm(2, 16, 32, 128), vm(2, 15, 32, 128), vm(2, 32, 128, dtype=F32),
        sems((7,)), sems((4,)), sems,
        sems((4,)), sems((4,)), sems((4, 4)), sems((4, 4)), sems((4, 4)), sems((4, 4)),
        sems((4, 4)), sems((4, 4)), sems((4, 7)), sems((4, 7)), sems((2, 2)), sems((2, 2)),
        sems((2, 3)), sems((2, 3)), sems((2, 3)), sems((2, 3)), sems((2, 15)), sems((2, 15)),
    ]
    anywhere = pl.BlockSpec(memory_space=pl.ANY)
    block_out, tokens_grad, qkv_grad, sums = pl.pallas_call(
        kernel,
        out_shape=[
            jax.ShapeDtypeStruct((ROWS, D), BF), jax.ShapeDtypeStruct((ROWS, D), BF),
            jax.ShapeDtypeStruct((ROWS, 3 * HD), BF), jax.ShapeDtypeStruct((2, 32, 128), F32),
        ],
        in_specs=[anywhere] * 7,
        out_specs=[anywhere] * 4,
        scratch_shapes=scratch,
        compiler_params=pltpu.CompilerParams(
            collective_id=0, has_side_effects=True, vmem_limit_bytes=62 * 1024 * 1024
        ),
        name="block",
    )(
        tokens.reshape(ROWS, D), spatial_qkv.reshape(ROWS, 3 * HD), wo_spatial, w_temporal,
        wo_temporal, cotangent.reshape(ROWS, D), picker(),
    )
    return (
        block_out.reshape(frames, patches, D),
        tokens_grad.reshape(frames, patches, D),
        qkv_grad.reshape(frames, patches, 3 * HD),
        sums[0, :18, :72],
        sums[1, :18, :72],
    )


def solution(mesh):
    rows = P(("dp", "seq"), None, None)
    return jax.shard_map(
        shards,
        mesh=mesh,
        in_specs=(rows, rows, P(), P(None, "dp"), P(), rows),
        out_specs=(rows, rows, rows, P("seq", "dp"), P("seq", "dp")),
        check_vma=False,
    )
```

```python
import functools
import math

import jax
import jax.numpy as jnp
import numpy as np
from jax import lax
from jax.experimental import pallas as pl
from jax.experimental.pallas import tpu as pltpu
from jax.sharding import PartitionSpec as P

DH = 72
HEADS = 8
HD = 576
D = 1152
ROWS = 128
COLS = 108
SCALE = 1.0 / math.sqrt(DH)
MESH = pl.DeviceIdType.MESH
BF = jnp.bfloat16
F32 = jnp.float32


def device(y, zh, zl, x, core):
    return (y * 4 + zh, (zl * 4 + x) * 2 + core)


def nt(left, right):
    return lax.dot_general(left, right, (((1,), (1,)), ((), ())), preferred_element_type=F32)


def tn(left, right):
    return lax.dot_general(left, right, (((0,), (0,)), ((), ())), preferred_element_type=F32)


def nn(left, right):
    return jnp.dot(left, right, preferred_element_type=F32)


def head(ref, n):
    return ref[:, n * DH : (n + 1) * DH]


def attend(qkv_ref, mask, p_ref, out_ref, heads):
    for h in heads:
        scores = nt(head(qkv_ref, h), head(qkv_ref, HEADS + h)) * SCALE
        scores = jnp.where(mask, scores, -1e30)
        scores = jnp.exp(scores - jnp.max(scores, axis=-1, keepdims=True))
        weights = scores / jnp.sum(scores, axis=-1, keepdims=True)
        p_ref[h] = weights
        out = nn(weights.astype(BF), head(qkv_ref, 2 * HEADS + h))
        out_ref[:, h * DH : (h + 1) * DH] = out.astype(BF)


def attend_grad(qkv_ref, p_ref, g_ref, grad_ref, heads):
    for h in heads:
        weights = p_ref[h]
        grad = head(g_ref, h)
        value_grad = tn(weights.astype(BF), grad)
        weight_grad = nt(grad, head(qkv_ref, 2 * HEADS + h))
        centered = weight_grad - jnp.sum(weights * weight_grad, axis=-1, keepdims=True)
        score_grad = (weights * centered * SCALE).astype(BF)
        query_grad = nn(score_grad, head(qkv_ref, HEADS + h))
        key_grad = tn(score_grad, head(qkv_ref, h))
        for part, value in enumerate((query_grad, key_grad, value_grad)):
            at = (part * HEADS + h) * DH
            grad_ref[:, at : at + DH] = value.astype(BF)


def to_peers(value, send_ref):
    for j in range(8):
        block = jnp.concatenate([value[8 * j : 8 * j + 8], value[64 + 8 * j : 72 + 8 * j]], axis=0)
        send_ref[j] = block.astype(BF)


def from_peers(recv_ref):
    blocks = [recv_ref[j].astype(F32) for j in range(8)]
    return jnp.concatenate([b[:8] for b in blocks] + [b[8:] for b in blocks], axis=0)


def kernel(
    tokens_hbm, sqkv_hbm, wos_hbm, w_hbm, wot_hbm, cot_hbm, pick_hbm,
    block_hbm, tgrad_hbm, sgrad_hbm, sums_hbm,
    tok, sqkv, wos, wraw, wpad, wot, cot, pick, wbuf,
    hid, hid_s, hid_r, og_s, og_r, pg_s, pg_r, to_s, to_r,
    ps_ref, pt_ref, so, tqkv, tqkvp, to, og, dqkv, tgrad, sog, sgrad, block, trow,
    lt, ltx, rx, gsend, grecv, ysend, yrecv, zsend, zrecv, sums,
    load_sems, out_sems, own_sem,
    zss, zrs, fss, frs, sss, srs, css, crs, ass, ars, oss, ors, xss, xrs, yss, yrs, rss, rrs,
):
    dp, seq = lax.axis_index("dp"), lax.axis_index("seq")
    y, zh, zl, x, c = dp // 4, dp % 4, seq // 8, (seq // 2) % 4, seq % 2
    u = (1 - c) * y + c * x
    v = (1 - c) * x + c * y
    zpos = zh * 4 + zl

    def at(u_, v_):
        return device((1 - c) * u_ + c * v_, zh, zl, (1 - c) * v_ + c * u_, c)

    partner = device(y, zh, zl, x, 1 - c)
    me = x * 2 + c
    peers = [(me + d) % 8 for d in range(1, 8)]
    peer_ids = [device(y, zh, zl, j // 2, j % 2) for j in peers]
    y_ids = [device((y + d) % 4, zh, zl, x, c) for d in range(1, 4)]
    x_ids = [device(y, zh, zl, (x + d) % 4, c) for d in range(1, 4)]
    z_at = [(zpos + d) % 16 for d in range(1, 16)]
    z_ids = [device(y, z // 4, z % 4, x, c) for z in z_at]
    everyone = peer_ids + y_ids + z_ids

    barrier = pltpu.get_barrier_semaphore()
    for target in everyone:
        pl.semaphore_signal(barrier, inc=1, device_id=target, device_id_type=MESH)

    loads = {}
    for n, (name, src, dst) in enumerate(
        (
            ("w", w_hbm, wraw), ("sqkv", sqkv_hbm, sqkv), ("cot", cot_hbm, cot), ("wot", wot_hbm, wot),
            ("wos", wos_hbm, wos), ("tok", tokens_hbm, tok), ("pick", pick_hbm, pick),
        )
    ):
        loads[name] = pltpu.make_async_copy(src, dst, load_sems.at[n])
        loads[name].start()
    pending = []

    def send(src, dst, send_sem, recv_sem, target):
        copy = pltpu.make_async_remote_copy(
            src_ref=src, dst_ref=dst, send_sem=send_sem, recv_sem=recv_sem,
            device_id=target, device_id_type=MESH,
        )
        copy.start()
        pending.append(copy)
        return copy

    loads["w"].wait()
    turned = wraw[...].astype(F32).T.astype(BF)
    wpad[...] = jnp.concatenate([turned, jnp.zeros((D, 128 - COLS), BF)], axis=1)

    def ring(slot, low, high, pos, ids, ss, rs):
        state = {}

        def start():
            ref = slot(pos)
            state["up"] = send(ref, ref, ss.at[0], rs.at[0], ids[0])
            state["down"] = send(ref, ref, ss.at[1], rs.at[1], ids[2])

        def relay():
            state["up"].wait_recv()
            ref = low(slot((pos + 3) % 4))
            state["up2"] = send(ref, ref, ss.at[2], rs.at[2], ids[0])
            state["down"].wait_recv()
            ref = high(slot((pos + 1) % 4))
            state["down2"] = send(ref, ref, ss.at[3], rs.at[3], ids[2])

        def finish():
            state["up2"].wait_recv()
            state["down2"].wait_recv()

        return start, relay, finish

    def direct(slot, pos, ids, ss, rs):
        state = {}

        def start():
            ref = slot(pos)
            for d in (2, 1, 3):
                state[d] = send(ref, ref, ss.at[d - 1], rs.at[d - 1], ids[d - 1])

        def near():
            state[1].wait_recv()
            state[3].wait_recv()

        def far():
            state[2].wait_recv()

        return start, near, far

    zring_ids = [device(y, (zh + d) % 4, zl, x, c) for d in range(1, 4)]
    u_ids = [at((u + d) % 4, v) for d in range(1, 4)]
    v_ids = [at(u, (v + d) % 4) for d in range(1, 4)]
    zr = direct(lambda p: wbuf.at[p, c, v, u], zh, zring_ids, zss, zrs)
    order = (0, 1, 3, 2)
    zsets = [(zh + 4 - e) % 4 for e in order]
    fr = [
        direct(lambda p, s=s: wbuf.at[s, c, v, p], u, u_ids, fss.at[i], frs.at[i])
        for i, s in enumerate(zsets)
    ]
    sr = [
        ring(
            lambda p, s=s: wbuf.at[s, c, p], lambda r: r.at[pl.ds(0, 2)], lambda r: r.at[pl.ds(2, 2)],
            v, v_ids, sss.at[i], srs.at[i],
        )
        for i, s in enumerate(zsets[:3])
    ]
    sr.append(direct(lambda p: wbuf.at[zsets[3], c, p], v, v_ids, sss.at[3], srs.at[3]))
    crosses = {}

    def cross(i, d):
        ref = wbuf.at[zsets[i], c, (v + d) % 4]
        crosses[i, d] = send(ref, ref, css.at[i, d], crs.at[i, d], partner)

    def stage_c(i):
        fr[i][1]()
        fr[i][2]()
        sr[i][0]()
        cross(i, 0)

    def stage_d(i):
        sr[i][1]()
        cross(i, 3)
        cross(i, 1)

    def stage_e(i):
        sr[i][2]()
        cross(i, 2)

    def stage_f(i):
        for d in range(4):
            crosses[i, d].wait_recv()

    def gather():
        own = pltpu.make_async_copy(wpad.at[pl.ds((c * 4 + x) * 144, 144)], wbuf.at[zh, c, v, u], own_sem)
        own.start()
        own.wait()
        zr[0]()
        fr[0][0]()
        yield
        stage_c(0)
        yield
        stage_d(0)
        zr[1]()
        fr[1][0]()
        fr[2][0]()
        stage_e(0)
        stage_c(1)
        stage_c(2)
        zr[2]()
        fr[3][0]()
        stage_d(1)
        stage_d(2)
        stage_c(3)
        yield
        stage_f(0)
        yield
        stage_e(1)
        stage_f(1)
        yield
        stage_e(2)
        stage_f(2)
        yield
        stage_d(3)
        stage_e(3)
        stage_f(3)
        yield

    def exchange(n, src, dst):
        copies = []
        for d in (1, 7, 2, 6, 3, 5, 4):
            copies.append(
                send(src.at[peers[d - 1]], dst.at[me], ass.at[n, d - 1], ars.at[n, d - 1], peer_ids[d - 1])
            )
        dst[me] = src[me]
        return copies

    def arrived(copies):
        for copy in copies:
            copy.wait_recv()

    def weight_sum(w, left_ref, right_ref):
        lt[w] = nt(pick[...], left_ref[...]).astype(BF).reshape(2, 320, ROWS)
        swap = (
            send(lt.at[w, 1 - c], ltx.at[w], oss.at[w, 0], ors.at[w, 0], partner),
            send(right_ref, rx.at[w], oss.at[w, 1], ors.at[w, 1], partner),
        )
        yield
        arrived(swap)
        for xk in range(4):
            rows = pl.ds(xk * 80, 80)
            total = nn(lt[w, c, rows], right_ref[...]) + nn(ltx[w, rows], rx[w])
            for yk in range(4):
                gsend[w, (1 - c) * xk + c * yk, (1 - c) * yk + c * xk, :, 0:288] = total[
                    :, yk * 288 : (yk + 1) * 288
                ].astype(BF)
        first_at = (1 - c) * x + c * y
        second_at = (1 - c) * y + c * x

        def step_id(first, d):
            dx = (1 - c) * d if first else c * d
            dy = d - dx
            return device((y + dy) % 4, zh, zl, (x + dx) % 4, c)

        copies = [
            send(
                gsend.at[w, (first_at + d) % 4], grecv.at[w, d - 1], xss.at[w, d - 1], xrs.at[w, d - 1],
                step_id(True, d),
            )
            for d in (1, 3, 2)
        ]
        yield
        arrived(copies)
        for k in range(4):
            total = gsend[w, first_at, k].astype(F32)
            for d in range(3):
                total += grecv[w, d, k].astype(F32)
            ysend[w, k] = total.astype(BF)
        copies = [
            send(
                ysend.at[w, (second_at + d) % 4], yrecv.at[w, d - 1], yss.at[w, d - 1], yrs.at[w, d - 1],
                step_id(False, d),
            )
            for d in (1, 3, 2)
        ]
        yield
        arrived(copies)
        total = ysend[w, second_at].astype(F32)
        for d in range(3):
            total += yrecv[w, d].astype(F32)
        for zh_ in range(4):
            for zl_ in range(4):
                zsend[w, zh_ * 4 + zl_, 0:18, 0:72] = total[
                    zl_ * 18 : (zl_ + 1) * 18, zh_ * 72 : (zh_ + 1) * 72
                ].astype(BF)
        copies = [
            send(
                zsend.at[w, z_at[d - 1]], zrecv.at[w, d - 1], rss.at[w, d - 1], rrs.at[w, d - 1], z_ids[d - 1]
            )
            for d in range(1, 16)
        ]
        yield
        arrived(copies)
        total = zsend[w, zpos].astype(F32)
        for d in range(15):
            total += zrecv[w, d].astype(F32)
        sums[w] = total
        yield

    row = lax.broadcasted_iota(jnp.int32, (ROWS, ROWS), 0)
    col = lax.broadcasted_iota(jnp.int32, (ROWS, ROWS), 1)
    same_frame = (row // 64) == (col // 64)
    same_patch = (row % 8) == (col % 8)

    loads["cot"].wait()
    loads["wot"].wait()
    to_peers(nt(cot[...], wot[...]), og_s)
    loads["sqkv"].wait()

    attend(sqkv, same_frame, ps_ref, so, range(8))
    loads["wos"].wait()
    loads["tok"].wait()
    loads["pick"].wait()
    hidden = tok[...].astype(F32) + nn(so[...], wos[...])
    hid[...] = hidden.astype(BF)
    to_peers(hidden, hid_s)

    pl.semaphore_wait(barrier, len(everyone))
    steps = gather()
    next(steps)
    hidden_copies = exchange(0, hid_s, hid_r)
    next(steps)
    next(steps)
    grad_copies = exchange(1, og_s, og_r)
    arrived(hidden_copies)

    def shard_of(s, y_):
        upper = wbuf[s, 0, :, y_].reshape(HD, 128)
        lower = wbuf[s, 1, y_].reshape(HD, 128)
        return jnp.concatenate([upper, lower], axis=0)

    def project(i):
        rows = hid_r[...].reshape(ROWS, D)
        for pair in range(2):
            both = jnp.concatenate([shard_of(zsets[i], 2 * pair), shard_of(zsets[i], 2 * pair + 1)], axis=1)
            out = nn(rows, both).astype(BF)
            for k in range(2):
                tqkvp[(2 * pair + k) * 4 + zsets[i]] = out[:, k * 128 : (k + 1) * 128]

    for i in range(4):
        next(steps)
        project(i)
    for s in range(16):
        tqkv[:, s * COLS : (s + 1) * COLS] = tqkvp[s, :, 0:COLS]

    attend(tqkv, same_patch, pt_ref, to, range(8))
    to_s[...] = to[...].reshape(8, 16, HD)
    out_copies = exchange(2, to_s, to_r)
    arrived(grad_copies)
    og[...] = og_r[...].reshape(ROWS, HD)
    attend_grad(tqkv, pt_ref, og, dqkv, range(8))
    total = None
    for pair in range(8):
        grads, weights = [], []
        for k in range(2):
            s = 2 * pair + k
            grads += [dqkv[:, s * COLS : (s + 1) * COLS], jnp.zeros((ROWS, 128 - COLS), BF)]
            weights.append(shard_of(s % 4, s // 4))
        part = nt(jnp.concatenate(grads, axis=1), jnp.concatenate(weights, axis=1))
        total = part if total is None else total + part
    pg_s[...] = total.astype(BF).reshape(8, 16, D)
    projection_copies = exchange(3, pg_s, pg_r)

    arrived(out_copies)
    rows = from_peers(to_r).astype(BF)
    trow[...] = rows
    temporal_sum = weight_sum(1, trow, cot)
    next(temporal_sum)
    block[...] = (hid[...].astype(F32) + nn(rows, wot[...])).astype(BF)
    outs = [pltpu.make_async_copy(block, block_hbm, out_sems.at[0])]
    outs[0].start()
    next(temporal_sum)
    arrived(projection_copies)
    tgrad[...] = (cot[...].astype(F32) + from_peers(pg_r)).astype(BF)
    outs.append(pltpu.make_async_copy(tgrad, tgrad_hbm, out_sems.at[1]))
    outs[1].start()
    spatial_sum = weight_sum(0, so, tgrad)
    next(spatial_sum)
    sog[...] = nt(tgrad[...], wos[...]).astype(BF)
    next(spatial_sum)
    next(temporal_sum)
    attend_grad(sqkv, ps_ref, sog, sgrad, range(0, 4))
    next(temporal_sum)
    attend_grad(sqkv, ps_ref, sog, sgrad, range(4, 8))
    outs.append(pltpu.make_async_copy(sgrad, sgrad_hbm, out_sems.at[2]))
    outs[2].start()
    next(spatial_sum)
    next(spatial_sum)
    next(temporal_sum)
    next(spatial_sum)
    outs.append(pltpu.make_async_copy(sums, sums_hbm, out_sems.at[3]))
    outs[3].start()
    for copy in outs:
        copy.wait()
    for copy in pending:
        copy.wait_send()


def finish_kernel(
    block_hbm, tgrad_hbm, sgrad_hbm, sums_hbm, o1, o2, o3, o4, o5, block, tgrad, sgrad, sums, s1, s2, in_sems, out_sems
):
    ins = [
        pltpu.make_async_copy(src, dst, in_sems.at[n])
        for n, (src, dst) in enumerate(
            ((sums_hbm, sums), (block_hbm, block), (tgrad_hbm, tgrad), (sgrad_hbm, sgrad))
        )
    ]
    for copy in ins:
        copy.start()
    ins[0].wait()
    s1[...] = sums[0, 0:18, 0:72]
    s2[...] = sums[1, 0:18, 0:72]
    outs = []
    for n, (src, dst) in enumerate(((s1, o4), (s2, o5), (block, o1), (tgrad, o2), (sgrad, o3))):
        if n >= 2:
            ins[n - 1].wait()
        outs.append(pltpu.make_async_copy(src, dst, out_sems.at[n]))
        outs[-1].start()
    for copy in outs:
        copy.wait()


def picker():
    pick = np.zeros((2, 4, 80, HD), np.float32)
    for zl in range(4):
        for x in range(4):
            for core in range(2):
                for i in range(18):
                    pick[core, x, zl * 18 + i, ((zl * 4 + x) * 2 + core) * 18 + i] = 1
    return jnp.asarray(pick.reshape(640, HD), BF)


def shards(tokens, spatial_qkv, wo_spatial, w_temporal, wo_temporal, cotangent):
    frames, patches, _ = tokens.shape
    sems = pltpu.SemaphoreType.DMA

    def vm(*shape, dtype=BF):
        return pltpu.VMEM(shape, dtype)

    scratch = [
        vm(ROWS, D), vm(ROWS, 3 * HD), vm(HD, D), vm(COLS, D), vm(D, 128), vm(HD, D), vm(ROWS, D),
        vm(640, HD), vm(4, 2, 4, 4, 144, 128),
        vm(ROWS, D), vm(8, 16, D), vm(8, 16, D), vm(8, 16, HD), vm(8, 16, HD),
        vm(8, 16, D), vm(8, 16, D), vm(8, 16, HD), vm(8, 16, HD),
        vm(8, ROWS, ROWS, dtype=F32), vm(8, ROWS, ROWS, dtype=F32),
        vm(ROWS, HD), vm(ROWS, 3 * HD), vm(16, ROWS, 128), vm(ROWS, HD), vm(ROWS, HD),
        vm(ROWS, 3 * HD), vm(ROWS, D), vm(ROWS, HD), vm(ROWS, 3 * HD), vm(ROWS, D), vm(ROWS, HD),
        vm(2, 2, 320, ROWS), vm(2, 320, ROWS), vm(2, ROWS, D),
        vm(2, 4, 4, 80, 384), vm(2, 3, 4, 80, 384), vm(2, 4, 80, 384), vm(2, 3, 80, 384),
        vm(2, 16, 32, 128), vm(2, 15, 32, 128), vm(2, 32, 128, dtype=F32),
        sems((7,)), sems((4,)), sems,
        sems((4,)), sems((4,)), sems((4, 4)), sems((4, 4)), sems((4, 4)), sems((4, 4)),
        sems((4, 4)), sems((4, 4)), sems((4, 7)), sems((4, 7)), sems((2, 2)), sems((2, 2)),
        sems((2, 3)), sems((2, 3)), sems((2, 3)), sems((2, 3)), sems((2, 15)), sems((2, 15)),
    ]
    anywhere = pl.BlockSpec(memory_space=pl.ANY)
    block_out, tokens_grad, qkv_grad, sums = pl.pallas_call(
        kernel,
        out_shape=[
            jax.ShapeDtypeStruct((ROWS, D), BF), jax.ShapeDtypeStruct((ROWS, D), BF),
            jax.ShapeDtypeStruct((ROWS, 3 * HD), BF), jax.ShapeDtypeStruct((2, 32, 128), F32),
        ],
        in_specs=[anywhere] * 7,
        out_specs=[anywhere] * 4,
        scratch_shapes=scratch,
        compiler_params=pltpu.CompilerParams(
            collective_id=0, has_side_effects=True, vmem_limit_bytes=62 * 1024 * 1024
        ),
        name="block",
    )(
        tokens.reshape(ROWS, D), spatial_qkv.reshape(ROWS, 3 * HD), wo_spatial, w_temporal.T,
        wo_temporal, cotangent.reshape(ROWS, D), picker(),
    )
    block_out, tokens_grad, qkv_grad, spatial_sum, temporal_sum = pl.pallas_call(
        finish_kernel,
        out_shape=[
            jax.ShapeDtypeStruct((ROWS, D), BF), jax.ShapeDtypeStruct((ROWS, D), BF),
            jax.ShapeDtypeStruct((ROWS, 3 * HD), BF),
            jax.ShapeDtypeStruct((18, 72), F32), jax.ShapeDtypeStruct((18, 72), F32),
        ],
        in_specs=[anywhere] * 4,
        out_specs=[anywhere] * 5,
        scratch_shapes=[
            vm(ROWS, D), vm(ROWS, D), vm(ROWS, 3 * HD), vm(2, 32, 128, dtype=F32),
            vm(18, 72, dtype=F32), vm(18, 72, dtype=F32), sems((4,)), sems((5,)),
        ],
        name="finish",
    )(block_out, tokens_grad, qkv_grad, sums)
    return (
        block_out.reshape(frames, patches, D),
        tokens_grad.reshape(frames, patches, D),
        qkv_grad.reshape(frames, patches, 3 * HD),
        spatial_sum,
        temporal_sum,
    )


def solution(mesh):
    rows = P(("dp", "seq"), None, None)
    return jax.shard_map(
        shards,
        mesh=mesh,
        in_specs=(rows, rows, P(), P(None, "dp"), P(), rows),
        out_specs=(rows, rows, rows, P("seq", "dp"), P("seq", "dp")),
        check_vma=False,
    )
```

```python
import functools
import math

import jax
import jax.numpy as jnp
import numpy as np
from jax import lax
from jax.experimental import pallas as pl
from jax.experimental.pallas import tpu as pltpu
from jax.sharding import PartitionSpec as P

DH = 72
HEADS = 8
HD = 576
D = 1152
ROWS = 128
COLS = 108
SCALE = 1.0 / math.sqrt(DH)
MESH = pl.DeviceIdType.MESH
BF = jnp.bfloat16
F32 = jnp.float32


def device(y, zh, zl, x, core):
    return (y * 4 + zh, (zl * 4 + x) * 2 + core)


def nt(left, right):
    return lax.dot_general(left, right, (((1,), (1,)), ((), ())), preferred_element_type=F32)


def tn(left, right):
    return lax.dot_general(left, right, (((0,), (0,)), ((), ())), preferred_element_type=F32)


def nn(left, right):
    return jnp.dot(left, right, preferred_element_type=F32)


def head(ref, n):
    return ref[:, n * DH : (n + 1) * DH]


def attend(qkv_ref, mask, p_ref, out_ref, heads):
    for h in heads:
        scores = nt(head(qkv_ref, h), head(qkv_ref, HEADS + h)) * SCALE
        scores = jnp.where(mask, scores, -1e30)
        scores = jnp.exp(scores - jnp.max(scores, axis=-1, keepdims=True))
        weights = scores / jnp.sum(scores, axis=-1, keepdims=True)
        p_ref[h] = weights
        out = nn(weights.astype(BF), head(qkv_ref, 2 * HEADS + h))
        out_ref[:, h * DH : (h + 1) * DH] = out.astype(BF)


def attend_grad(qkv_ref, p_ref, g_ref, grad_ref, heads):
    for h in heads:
        weights = p_ref[h]
        grad = head(g_ref, h)
        value_grad = tn(weights.astype(BF), grad)
        weight_grad = nt(grad, head(qkv_ref, 2 * HEADS + h))
        centered = weight_grad - jnp.sum(weights * weight_grad, axis=-1, keepdims=True)
        score_grad = (weights * centered * SCALE).astype(BF)
        query_grad = nn(score_grad, head(qkv_ref, HEADS + h))
        key_grad = tn(score_grad, head(qkv_ref, h))
        for part, value in enumerate((query_grad, key_grad, value_grad)):
            at = (part * HEADS + h) * DH
            grad_ref[:, at : at + DH] = value.astype(BF)


def to_peers(value, send_ref):
    for j in range(8):
        block = jnp.concatenate([value[8 * j : 8 * j + 8], value[64 + 8 * j : 72 + 8 * j]], axis=0)
        send_ref[j] = block.astype(BF)


def from_peers(recv_ref):
    blocks = [recv_ref[j].astype(F32) for j in range(8)]
    return jnp.concatenate([b[:8] for b in blocks] + [b[8:] for b in blocks], axis=0)


def kernel(
    tokens_hbm, sqkv_hbm, wos_hbm, w_hbm, wot_hbm, cot_hbm, pick_hbm,
    block_hbm, tgrad_hbm, sgrad_hbm, sums_hbm,
    tok, sqkv, wos, wraw, wpad, wot, cot, pick, wbuf,
    hid, hid_s, hid_r, cot_s, cot_r, tg_s, tg_r, to_s, to_r,
    ps_ref, pt_ref, so, tqkv, tqkvp, to, og, dqkv, tgrad, sog, sgrad, block,
    so_s, so_r, cotx, tgx, lt, ltx, gsend, grecv, ysend, yrecv, zsend, zrecv, sums,
    load_sems, out_sems, own_sem,
    zss, zrs, fss, frs, sss, srs, css, crs, ass, ars, oss, ors, xss, xrs, yss, yrs, rss, rrs,
):
    dp, seq = lax.axis_index("dp"), lax.axis_index("seq")
    y, zh, zl, x, c = dp // 4, dp % 4, seq // 8, (seq // 2) % 4, seq % 2
    u = (1 - c) * y + c * x
    v = (1 - c) * x + c * y
    zpos = zh * 4 + zl

    def at(u_, v_):
        return device((1 - c) * u_ + c * v_, zh, zl, (1 - c) * v_ + c * u_, c)

    partner = device(y, zh, zl, x, 1 - c)
    me = x * 2 + c
    peers = [(me + d) % 8 for d in range(1, 8)]
    peer_ids = [device(y, zh, zl, j // 2, j % 2) for j in peers]
    y_ids = [device((y + d) % 4, zh, zl, x, c) for d in range(1, 4)]
    x_ids = [device(y, zh, zl, (x + d) % 4, c) for d in range(1, 4)]
    z_at = [(zpos + d) % 16 for d in range(1, 16)]
    z_ids = [device(y, z // 4, z % 4, x, c) for z in z_at]
    everyone = peer_ids + y_ids + z_ids

    barrier = pltpu.get_barrier_semaphore()
    for target in everyone:
        pl.semaphore_signal(barrier, inc=1, device_id=target, device_id_type=MESH)

    loads = {}
    for n, (name, src, dst) in enumerate(
        (
            ("w", w_hbm, wraw), ("sqkv", sqkv_hbm, sqkv), ("cot", cot_hbm, cot), ("wot", wot_hbm, wot),
            ("wos", wos_hbm, wos), ("tok", tokens_hbm, tok), ("pick", pick_hbm, pick),
        )
    ):
        loads[name] = pltpu.make_async_copy(src, dst, load_sems.at[n])
        loads[name].start()
    pending = []

    def send(src, dst, send_sem, recv_sem, target):
        copy = pltpu.make_async_remote_copy(
            src_ref=src, dst_ref=dst, send_sem=send_sem, recv_sem=recv_sem,
            device_id=target, device_id_type=MESH,
        )
        copy.start()
        pending.append(copy)
        return copy

    loads["w"].wait()
    turned = wraw[...].astype(F32).T.astype(BF)
    wpad[...] = jnp.concatenate([turned, jnp.zeros((D, 128 - COLS), BF)], axis=1)
    own = pltpu.make_async_copy(wpad.at[pl.ds((c * 4 + x) * 144, 144)], wbuf.at[zh, c, v, u], own_sem)
    own.start()

    def ring(slot, low, high, pos, ids, ss, rs):
        state = {}

        def start():
            ref = slot(pos)
            state["up"] = send(ref, ref, ss.at[0], rs.at[0], ids[0])
            state["down"] = send(ref, ref, ss.at[1], rs.at[1], ids[2])

        def relay():
            state["up"].wait_recv()
            ref = low(slot((pos + 3) % 4))
            state["up2"] = send(ref, ref, ss.at[2], rs.at[2], ids[0])
            state["down"].wait_recv()
            ref = high(slot((pos + 1) % 4))
            state["down2"] = send(ref, ref, ss.at[3], rs.at[3], ids[2])

        def finish():
            state["up2"].wait_recv()
            state["down2"].wait_recv()

        return start, relay, finish

    def direct(slot, pos, ids, ss, rs):
        state = {}

        def start():
            ref = slot(pos)
            for d in (2, 1, 3):
                state[d] = send(ref, ref, ss.at[d - 1], rs.at[d - 1], ids[d - 1])

        def near():
            state[1].wait_recv()
            state[3].wait_recv()

        def far():
            state[2].wait_recv()

        return start, near, far

    zring_ids = [device(y, (zh + d) % 4, zl, x, c) for d in range(1, 4)]
    u_ids = [at((u + d) % 4, v) for d in range(1, 4)]
    v_ids = [at(u, (v + d) % 4) for d in range(1, 4)]
    zr = direct(lambda p: wbuf.at[p, c, v, u], zh, zring_ids, zss, zrs)
    order = (0, 1, 3, 2)
    zsets = [(zh + 4 - e) % 4 for e in order]
    fr = [
        direct(lambda p, s=s: wbuf.at[s, c, v, p], u, u_ids, fss.at[i], frs.at[i])
        for i, s in enumerate(zsets)
    ]
    sr = [
        ring(
            lambda p, s=s: wbuf.at[s, c, p], lambda r: r.at[pl.ds(0, 2)], lambda r: r.at[pl.ds(2, 2)],
            v, v_ids, sss.at[i], srs.at[i],
        )
        for i, s in enumerate(zsets)
    ]

    crosses = {}

    def cross(i, d):
        ref = wbuf.at[zsets[i], c, (v + d) % 4]
        crosses[i, d] = send(ref, ref, css.at[i, d], crs.at[i, d], partner)

    def stage_c(i):
        fr[i][1]()
        fr[i][2]()
        sr[i][0]()
        cross(i, 0)

    def stage_d(i):
        sr[i][1]()
        cross(i, 3)
        cross(i, 1)

    def stage_e(i):
        sr[i][2]()
        cross(i, 2)

    def stage_f(i):
        for d in range(4):
            crosses[i, d].wait_recv()

    def gather():
        zr[0]()
        fr[0][0]()
        stage_c(0)
        zr[1]()
        fr[1][0]()
        fr[2][0]()
        stage_d(0)
        zr[2]()
        fr[3][0]()
        stage_c(1)
        stage_c(2)
        yield
        stage_e(0)
        stage_c(3)
        stage_d(1)
        stage_d(2)
        stage_d(3)
        yield
        stage_f(0)
        yield
        stage_e(1)
        stage_e(2)
        stage_f(1)
        yield
        stage_f(2)
        yield
        stage_e(3)
        stage_f(3)
        yield

    def exchange(n, src, dst):
        copies = []
        for d in (1, 7, 2, 6, 3, 5, 4):
            copies.append(
                send(src.at[peers[d - 1]], dst.at[me], ass.at[n, d - 1], ars.at[n, d - 1], peer_ids[d - 1])
            )
        dst[me] = src[me]
        return copies

    def arrived(copies):
        for copy in copies:
            copy.wait_recv()

    def left_operand(n, value):
        lt[n] = nt(pick[...], value).astype(BF).reshape(2, 320, ROWS)
        return send(lt.at[n, 1 - c], ltx.at[n], oss.at[n], ors.at[n], partner)

    def weight_sum(w, product):
        for xk in range(4):
            total = product(pl.ds(xk * 80, 80), xk)
            for yk in range(4):
                first, second = (1 - c) * xk + c * yk, (1 - c) * yk + c * xk
                for k in range(2):
                    at_ = yk * 288 + k * 128
                    gsend[w, first, 2 * second + k] = total[:, at_ : at_ + 128].astype(BF)
            rests = [total[:, yk * 288 + 256 : yk * 288 + 288].astype(BF) for yk in range(4)]

            @pl.when(c == 0)
            def _():
                for yk in range(4):
                    gsend[w, xk, 8, :, yk * 32 : yk * 32 + 32] = rests[yk]

            @pl.when(c == 1)
            def _():
                for yk in range(4):
                    gsend[w, yk, 8, :, xk * 32 : xk * 32 + 32] = rests[yk]

        yield
        first_at = (1 - c) * x + c * y
        second_at = (1 - c) * y + c * x

        def step_id(first, d):
            dx = (1 - c) * d if first else c * d
            dy = d - dx
            return device((y + dy) % 4, zh, zl, (x + dx) % 4, c)

        copies = [
            send(
                gsend.at[w, (first_at + d) % 4], grecv.at[w, d - 1], xss.at[w, d - 1], xrs.at[w, d - 1],
                step_id(True, d),
            )
            for d in (1, 3, 2)
        ]
        yield
        arrived(copies)

        def first_sum(k):
            total = gsend[w, first_at, k].astype(F32)
            for d in range(3):
                total += grecv[w, d, k].astype(F32)
            return total.astype(BF)

        rest = first_sum(8)
        for k in range(4):
            ysend[w, k, :, 0:128] = first_sum(2 * k)
            ysend[w, k, :, 128:256] = first_sum(2 * k + 1)
            ysend[w, k, :, 256:288] = rest[:, k * 32 : k * 32 + 32]
        copies = [
            send(
                ysend.at[w, (second_at + d) % 4], yrecv.at[w, d - 1], yss.at[w, d - 1], yrs.at[w, d - 1],
                step_id(False, d),
            )
            for d in (1, 3, 2)
        ]
        yield
        arrived(copies)
        total = ysend[w, second_at].astype(F32)
        for d in range(3):
            total += yrecv[w, d].astype(F32)
        for zh_ in range(4):
            for zl_ in range(4):
                zsend[w, zh_ * 4 + zl_, 0:18, 0:72] = total[
                    zl_ * 18 : (zl_ + 1) * 18, zh_ * 72 : (zh_ + 1) * 72
                ].astype(BF)
        copies = [
            send(
                zsend.at[w, z_at[d - 1]], zrecv.at[w, d - 1], rss.at[w, d - 1], rrs.at[w, d - 1], z_ids[d - 1]
            )
            for d in (8, 7, 9, 6, 10, 5, 11, 4, 12, 3, 13, 2, 14, 1, 15)
        ]
        yield
        arrived(copies)
        total = zsend[w, zpos].astype(F32)
        for d in range(15):
            total += zrecv[w, d].astype(F32)
        sums[w] = total
        yield

    row = lax.broadcasted_iota(jnp.int32, (ROWS, ROWS), 0)
    col = lax.broadcasted_iota(jnp.int32, (ROWS, ROWS), 1)
    same_frame = (row // 64) == (col // 64)
    same_patch = (row % 8) == (col % 8)

    loads["cot"].wait()
    to_peers(cot[...].astype(F32), cot_s)
    loads["sqkv"].wait()

    attend(sqkv, same_frame, ps_ref, so, range(8))
    loads["wos"].wait()
    loads["tok"].wait()
    loads["pick"].wait()
    loads["wot"].wait()
    hidden = tok[...].astype(F32) + nn(so[...], wos[...])
    hid[...] = hidden.astype(BF)
    to_peers(so[...].astype(F32), so_s)
    to_peers(hidden, hid_s)

    own.wait()
    pl.semaphore_wait(barrier, len(everyone))
    steps = gather()
    next(steps)
    hidden_copies = exchange(0, hid_s, hid_r)
    next(steps)
    cot_copies = exchange(1, cot_s, cot_r)
    spatial_copies = exchange(4, so_s, so_r)
    arrived(hidden_copies)

    def shard_of(s, y_):
        upper = wbuf[s, 0, :, y_].reshape(HD, 128)
        lower = wbuf[s, 1, y_].reshape(HD, 128)
        return jnp.concatenate([upper, lower], axis=0)

    def project(i):
        rows = hid_r[...].reshape(ROWS, D)
        for pair in range(2):
            both = jnp.concatenate([shard_of(zsets[i], 2 * pair), shard_of(zsets[i], 2 * pair + 1)], axis=1)
            out = nn(rows, both).astype(BF)
            for k in range(2):
                tqkvp[(2 * pair + k) * 4 + zsets[i]] = out[:, k * 128 : (k + 1) * 128]

    for i in range(4):
        next(steps)
        project(i)
    for s in range(16):
        tqkv[:, s * COLS : (s + 1) * COLS] = tqkvp[s, :, 0:COLS]

    arrived(cot_copies)
    cot_swap = send(cot_r, cotx, oss.at[2], ors.at[2], partner)
    attend(tqkv, same_patch, pt_ref, to, range(8))
    to_s[...] = to[...].reshape(8, 16, HD)
    out_copies = exchange(2, to_s, to_r)
    temporal_left = left_operand(1, to[...])
    og[...] = nt(cot_r[...].reshape(ROWS, D), wot[...]).astype(BF)
    arrived(spatial_copies)
    spatial_left = left_operand(0, so_r[...].reshape(ROWS, HD))
    attend_grad(tqkv, pt_ref, og, dqkv, range(8))

    def temporal_product(part, xk):
        mine = nn(lt[1, c, part], cot_r[...].reshape(ROWS, D))
        return mine + nn(ltx[1, part], cotx[...].reshape(ROWS, D))

    def spatial_product(part, xk):
        mine = nn(lt[0, c, part], tg_s[...].reshape(ROWS, D))
        return mine + nn(ltx[0, part], tgx[...].reshape(ROWS, D))

    temporal_sum = weight_sum(1, temporal_product)
    spatial_sum = weight_sum(0, spatial_product)
    arrived((temporal_left, cot_swap))
    next(temporal_sum)
    next(temporal_sum)
    total = None
    for pair in range(8):
        grads, weights = [], []
        for k in range(2):
            s = 2 * pair + k
            grads += [dqkv[:, s * COLS : (s + 1) * COLS], jnp.zeros((ROWS, 128 - COLS), BF)]
            weights.append(shard_of(s % 4, s // 4))
        part = nt(jnp.concatenate(grads, axis=1), jnp.concatenate(weights, axis=1))
        total = part if total is None else total + part
    total = cot_r[...].reshape(ROWS, D).astype(F32) + total.astype(BF).astype(F32)
    tg_s[...] = total.astype(BF).reshape(8, 16, D)
    tg_swap = send(tg_s, tgx, oss.at[3], ors.at[3], partner)
    tokens_copies = exchange(3, tg_s, tg_r)
    arrived((tg_swap, spatial_left))
    next(spatial_sum)
    next(spatial_sum)

    arrived(out_copies)
    block[...] = (hid[...].astype(F32) + nn(from_peers(to_r).astype(BF), wot[...])).astype(BF)
    outs = [pltpu.make_async_copy(block, block_hbm, out_sems.at[0])]
    outs[0].start()
    next(temporal_sum)
    arrived(tokens_copies)
    tgrad[...] = from_peers(tg_r).astype(BF)
    outs.append(pltpu.make_async_copy(tgrad, tgrad_hbm, out_sems.at[1]))
    outs[1].start()
    sog[...] = nt(tgrad[...], wos[...]).astype(BF)
    next(temporal_sum)
    next(spatial_sum)
    attend_grad(sqkv, ps_ref, sog, sgrad, range(0, 4))
    next(spatial_sum)
    attend_grad(sqkv, ps_ref, sog, sgrad, range(4, 8))
    outs.append(pltpu.make_async_copy(sgrad, sgrad_hbm, out_sems.at[2]))
    outs[2].start()
    next(temporal_sum)
    next(spatial_sum)
    outs.append(pltpu.make_async_copy(sums, sums_hbm, out_sems.at[3]))
    outs[3].start()
    for copy in outs:
        copy.wait()
    for copy in pending:
        copy.wait_send()


def finish_kernel(
    block_hbm, tgrad_hbm, sgrad_hbm, sums_hbm, o1, o2, o3, o4, o5, block, tgrad, sgrad, sums, s1, s2, in_sems, out_sems
):
    ins = [
        pltpu.make_async_copy(src, dst, in_sems.at[n])
        for n, (src, dst) in enumerate(
            ((sums_hbm, sums), (block_hbm, block), (tgrad_hbm, tgrad), (sgrad_hbm, sgrad))
        )
    ]
    for copy in ins:
        copy.start()
    ins[0].wait()
    s1[...] = sums[0, 0:18, 0:72]
    s2[...] = sums[1, 0:18, 0:72]
    outs = []
    for n, (src, dst) in enumerate(((s1, o4), (s2, o5), (block, o1), (tgrad, o2), (sgrad, o3))):
        if n >= 2:
            ins[n - 1].wait()
        outs.append(pltpu.make_async_copy(src, dst, out_sems.at[n]))
        outs[-1].start()
    for copy in outs:
        copy.wait()


def picker():
    pick = np.zeros((2, 4, 80, HD), np.float32)
    for zl in range(4):
        for x in range(4):
            for core in range(2):
                for i in range(18):
                    pick[core, x, zl * 18 + i, ((zl * 4 + x) * 2 + core) * 18 + i] = 1
    return jnp.asarray(pick.reshape(640, HD), BF)


def shards(tokens, spatial_qkv, wo_spatial, w_temporal, wo_temporal, cotangent):
    frames, patches, _ = tokens.shape
    sems = pltpu.SemaphoreType.DMA

    def vm(*shape, dtype=BF):
        return pltpu.VMEM(shape, dtype)

    scratch = [
        vm(ROWS, D), vm(ROWS, 3 * HD), vm(HD, D), vm(COLS, D), vm(D, 128), vm(HD, D), vm(ROWS, D),
        vm(640, HD), vm(4, 2, 4, 4, 144, 128),
        vm(ROWS, D), vm(8, 16, D), vm(8, 16, D), vm(8, 16, D), vm(8, 16, D),
        vm(8, 16, D), vm(8, 16, D), vm(8, 16, HD), vm(8, 16, HD),
        vm(8, ROWS, ROWS, dtype=F32), vm(8, ROWS, ROWS, dtype=F32),
        vm(ROWS, HD), vm(ROWS, 3 * HD), vm(16, ROWS, 128), vm(ROWS, HD), vm(ROWS, HD),
        vm(ROWS, 3 * HD), vm(ROWS, D), vm(ROWS, HD), vm(ROWS, 3 * HD), vm(ROWS, D),
        vm(8, 16, HD), vm(8, 16, HD), vm(8, 16, D), vm(8, 16, D),
        vm(2, 2, 320, ROWS), vm(2, 320, ROWS),
        vm(2, 4, 9, 80, 128), vm(2, 3, 9, 80, 128), vm(2, 4, 80, 384), vm(2, 3, 80, 384),
        vm(2, 16, 32, 128), vm(2, 15, 32, 128), vm(2, 32, 128, dtype=F32),
        sems((7,)), sems((4,)), sems,
        sems((4,)), sems((4,)), sems((4, 4)), sems((4, 4)), sems((4, 4)), sems((4, 4)),
        sems((4, 4)), sems((4, 4)), sems((5, 7)), sems((5, 7)), sems((4,)), sems((4,)),
        sems((2, 3)), sems((2, 3)), sems((2, 3)), sems((2, 3)), sems((2, 15)), sems((2, 15)),
    ]
    anywhere = pl.BlockSpec(memory_space=pl.ANY)
    block_out, tokens_grad, qkv_grad, sums = pl.pallas_call(
        kernel,
        out_shape=[
            jax.ShapeDtypeStruct((ROWS, D), BF), jax.ShapeDtypeStruct((ROWS, D), BF),
            jax.ShapeDtypeStruct((ROWS, 3 * HD), BF), jax.ShapeDtypeStruct((2, 32, 128), F32),
        ],
        in_specs=[anywhere] * 7,
        out_specs=[anywhere] * 4,
        scratch_shapes=scratch,
        compiler_params=pltpu.CompilerParams(
            collective_id=0, has_side_effects=True, vmem_limit_bytes=62 * 1024 * 1024
        ),
        name="block",
    )(
        tokens.reshape(ROWS, D), spatial_qkv.reshape(ROWS, 3 * HD), wo_spatial, w_temporal.T,
        wo_temporal, cotangent.reshape(ROWS, D), picker(),
    )
    block_out, tokens_grad, qkv_grad, spatial_sum, temporal_sum = pl.pallas_call(
        finish_kernel,
        out_shape=[
            jax.ShapeDtypeStruct((ROWS, D), BF), jax.ShapeDtypeStruct((ROWS, D), BF),
            jax.ShapeDtypeStruct((ROWS, 3 * HD), BF),
            jax.ShapeDtypeStruct((18, 72), F32), jax.ShapeDtypeStruct((18, 72), F32),
        ],
        in_specs=[anywhere] * 4,
        out_specs=[anywhere] * 5,
        scratch_shapes=[
            vm(ROWS, D), vm(ROWS, D), vm(ROWS, 3 * HD), vm(2, 32, 128, dtype=F32),
            vm(18, 72, dtype=F32), vm(18, 72, dtype=F32), sems((4,)), sems((5,)),
        ],
        name="finish",
    )(block_out, tokens_grad, qkv_grad, sums)
    return (
        block_out.reshape(frames, patches, D),
        tokens_grad.reshape(frames, patches, D),
        qkv_grad.reshape(frames, patches, 3 * HD),
        spatial_sum,
        temporal_sum,
    )


def solution(mesh):
    rows = P(("dp", "seq"), None, None)
    return jax.shard_map(
        shards,
        mesh=mesh,
        in_specs=(rows, rows, P(), P(None, "dp"), P(), rows),
        out_specs=(rows, rows, rows, P("seq", "dp"), P("seq", "dp")),
        check_vma=False,
    )
```

```python
import functools
import math

import jax
import jax.numpy as jnp
import numpy as np
from jax import lax
from jax.experimental import pallas as pl
from jax.experimental.pallas import tpu as pltpu
from jax.sharding import PartitionSpec as P

DH = 72
HEADS = 8
HD = 576
D = 1152
ROWS = 128
COLS = 108
SCALE = 1.0 / math.sqrt(DH)
MESH = pl.DeviceIdType.MESH
BF = jnp.bfloat16
F32 = jnp.float32


def device(y, zh, zl, x, core):
    return (y * 4 + zh, (zl * 4 + x) * 2 + core)


def nt(left, right):
    return lax.dot_general(left, right, (((1,), (1,)), ((), ())), preferred_element_type=F32)


def tn(left, right):
    return lax.dot_general(left, right, (((0,), (0,)), ((), ())), preferred_element_type=F32)


def nn(left, right):
    return jnp.dot(left, right, preferred_element_type=F32)


def head(ref, n):
    return ref[:, n * DH : (n + 1) * DH]


def attend(qkv_ref, mask, p_ref, out_ref, heads):
    for h in heads:
        scores = nt(head(qkv_ref, h), head(qkv_ref, HEADS + h)) * SCALE
        scores = jnp.where(mask, scores, -1e30)
        scores = jnp.exp(scores - jnp.max(scores, axis=-1, keepdims=True))
        weights = scores / jnp.sum(scores, axis=-1, keepdims=True)
        p_ref[h] = weights
        out = nn(weights.astype(BF), head(qkv_ref, 2 * HEADS + h))
        out_ref[:, h * DH : (h + 1) * DH] = out.astype(BF)


def attend_grad(qkv_ref, p_ref, g_ref, grad_ref, heads):
    for h in heads:
        weights = p_ref[h]
        grad = head(g_ref, h)
        value_grad = tn(weights.astype(BF), grad)
        weight_grad = nt(grad, head(qkv_ref, 2 * HEADS + h))
        centered = weight_grad - jnp.sum(weights * weight_grad, axis=-1, keepdims=True)
        score_grad = (weights * centered * SCALE).astype(BF)
        query_grad = nn(score_grad, head(qkv_ref, HEADS + h))
        key_grad = tn(score_grad, head(qkv_ref, h))
        for part, value in enumerate((query_grad, key_grad, value_grad)):
            at = (part * HEADS + h) * DH
            grad_ref[:, at : at + DH] = value.astype(BF)


def to_peers(value, send_ref):
    for j in range(8):
        block = jnp.concatenate([value[8 * j : 8 * j + 8], value[64 + 8 * j : 72 + 8 * j]], axis=0)
        send_ref[j] = block.astype(BF)


def from_peers(recv_ref):
    blocks = [recv_ref[j].astype(F32) for j in range(8)]
    return jnp.concatenate([b[:8] for b in blocks] + [b[8:] for b in blocks], axis=0)


def kernel(
    tokens_hbm, sqkv_hbm, wos_hbm, w_hbm, wot_hbm, cot_hbm, pick_hbm,
    block_hbm, tgrad_hbm, sgrad_hbm, sums_hbm,
    tok, sqkv, wos, wraw, wpad, wot, cot, pick, wbuf,
    hid, hid_s, hid_r, cot_s, cot_r, tg_s, tg_r, to_s, to_r,
    ps_ref, pt_ref, so, tqkv, tqkvp, to, og, dqkv, tgrad, sog, sgrad, block,
    so_s, so_r, cotx, tgx, lt, ltx, gsend, grecv, ysend, yrecv, zsend, zrecv, sums,
    load_sems, out_sems, own_sem,
    zss, zrs, fss, frs, sss, srs, css, crs, ass, ars, oss, ors, xss, xrs, yss, yrs, rss, rrs,
):
    dp, seq = lax.axis_index("dp"), lax.axis_index("seq")
    y, zh, zl, x, c = dp // 4, dp % 4, seq // 8, (seq // 2) % 4, seq % 2
    u = (1 - c) * y + c * x
    v = (1 - c) * x + c * y
    zpos = zh * 4 + zl

    def at(u_, v_):
        return device((1 - c) * u_ + c * v_, zh, zl, (1 - c) * v_ + c * u_, c)

    partner = device(y, zh, zl, x, 1 - c)
    me = x * 2 + c
    peers = [(me + d) % 8 for d in range(1, 8)]
    peer_ids = [device(y, zh, zl, j // 2, j % 2) for j in peers]
    y_ids = [device((y + d) % 4, zh, zl, x, c) for d in range(1, 4)]
    x_ids = [device(y, zh, zl, (x + d) % 4, c) for d in range(1, 4)]
    z_at = [(zpos + d) % 16 for d in range(1, 16)]
    z_ids = [device(y, z // 4, z % 4, x, c) for z in z_at]
    everyone = peer_ids + y_ids + z_ids

    barrier = pltpu.get_barrier_semaphore()
    for target in everyone:
        pl.semaphore_signal(barrier, inc=1, device_id=target, device_id_type=MESH)

    loads = {}
    for n, (name, src, dst) in enumerate(
        (
            ("w", w_hbm, wraw), ("sqkv", sqkv_hbm, sqkv), ("cot", cot_hbm, cot), ("wot", wot_hbm, wot),
            ("wos", wos_hbm, wos), ("tok", tokens_hbm, tok), ("pick", pick_hbm, pick),
        )
    ):
        loads[name] = pltpu.make_async_copy(src, dst, load_sems.at[n])
        loads[name].start()
    pending = []

    def send(src, dst, send_sem, recv_sem, target):
        copy = pltpu.make_async_remote_copy(
            src_ref=src, dst_ref=dst, send_sem=send_sem, recv_sem=recv_sem,
            device_id=target, device_id_type=MESH,
        )
        copy.start()
        pending.append(copy)
        return copy

    loads["w"].wait()
    turned = wraw[...].astype(F32).T.astype(BF)
    wpad[...] = jnp.concatenate([turned, jnp.zeros((D, 128 - COLS), BF)], axis=1)
    own = pltpu.make_async_copy(wpad.at[pl.ds((c * 4 + x) * 144, 144)], wbuf.at[zh, c, v, u], own_sem)
    own.start()

    def ring(slot, low, high, pos, ids, ss, rs):
        state = {}

        def start():
            ref = slot(pos)
            state["up"] = send(ref, ref, ss.at[0], rs.at[0], ids[0])
            state["down"] = send(ref, ref, ss.at[1], rs.at[1], ids[2])

        def relay():
            state["up"].wait_recv()
            ref = low(slot((pos + 3) % 4))
            state["up2"] = send(ref, ref, ss.at[2], rs.at[2], ids[0])
            state["down"].wait_recv()
            ref = high(slot((pos + 1) % 4))
            state["down2"] = send(ref, ref, ss.at[3], rs.at[3], ids[2])

        def finish():
            state["up2"].wait_recv()
            state["down2"].wait_recv()

        return start, relay, finish

    def direct(slot, pos, ids, ss, rs):
        state = {}

        def start():
            ref = slot(pos)
            for d in (2, 1, 3):
                state[d] = send(ref, ref, ss.at[d - 1], rs.at[d - 1], ids[d - 1])

        def near():
            state[1].wait_recv()
            state[3].wait_recv()

        def far():
            state[2].wait_recv()

        return start, near, far

    zring_ids = [device(y, (zh + d) % 4, zl, x, c) for d in range(1, 4)]
    u_ids = [at((u + d) % 4, v) for d in range(1, 4)]
    v_ids = [at(u, (v + d) % 4) for d in range(1, 4)]
    zr = direct(lambda p: wbuf.at[p, c, v, u], zh, zring_ids, zss, zrs)
    order = (0, 1, 3, 2)
    zsets = [(zh + 4 - e) % 4 for e in order]
    fr = [
        direct(lambda p, s=s: wbuf.at[s, c, v, p], u, u_ids, fss.at[i], frs.at[i])
        for i, s in enumerate(zsets)
    ]
    sr = [
        ring(
            lambda p, s=s: wbuf.at[s, c, p], lambda r: r.at[pl.ds(0, 2)], lambda r: r.at[pl.ds(2, 2)],
            v, v_ids, sss.at[i], srs.at[i],
        )
        for i, s in enumerate(zsets)
    ]

    crosses = {}

    def cross(i, d):
        ref = wbuf.at[zsets[i], c, (v + d) % 4]
        crosses[i, d] = send(ref, ref, css.at[i, d], crs.at[i, d], partner)

    def stage_c(i):
        fr[i][1]()
        fr[i][2]()
        sr[i][0]()
        cross(i, 0)

    def stage_d(i):
        sr[i][1]()
        cross(i, 3)
        cross(i, 1)

    def stage_e(i):
        sr[i][2]()
        cross(i, 2)

    def stage_f(i):
        for d in range(4):
            crosses[i, d].wait_recv()

    def gather():
        zr[0]()
        fr[0][0]()
        stage_c(0)
        zr[1]()
        fr[1][0]()
        fr[2][0]()
        stage_d(0)
        zr[2]()
        fr[3][0]()
        stage_c(1)
        stage_c(2)
        yield
        stage_e(0)
        stage_c(3)
        stage_d(1)
        stage_d(2)
        stage_d(3)
        yield
        stage_f(0)
        yield
        stage_e(1)
        stage_e(2)
        stage_f(1)
        yield
        stage_f(2)
        yield
        stage_e(3)
        stage_f(3)
        yield

    def exchange(n, src, dst):
        copies = []
        for d in (4, 3, 5, 2, 6, 1, 7):
            copies.append(
                send(src.at[peers[d - 1]], dst.at[me], ass.at[n, d - 1], ars.at[n, d - 1], peer_ids[d - 1])
            )
        dst[me] = src[me]
        return copies

    def arrived(copies):
        for copy in copies:
            copy.wait_recv()

    def left_operand(n, value):
        lt[n] = nt(pick[...], value).astype(BF).reshape(2, 320, ROWS)
        return send(lt.at[n, 1 - c], ltx.at[n], oss.at[n], ors.at[n], partner)

    def weight_sum(w, product):
        for xk in range(4):
            total = product(pl.ds(xk * 80, 80), xk)
            for yk in range(4):
                first, second = (1 - c) * xk + c * yk, (1 - c) * yk + c * xk
                for k in range(2):
                    at_ = yk * 288 + k * 128
                    gsend[w, first, 2 * second + k] = total[:, at_ : at_ + 128].astype(BF)
            rests = [total[:, yk * 288 + 256 : yk * 288 + 288].astype(BF) for yk in range(4)]

            @pl.when(c == 0)
            def _():
                for yk in range(4):
                    gsend[w, xk, 8, :, yk * 32 : yk * 32 + 32] = rests[yk]

            @pl.when(c == 1)
            def _():
                for yk in range(4):
                    gsend[w, yk, 8, :, xk * 32 : xk * 32 + 32] = rests[yk]

        yield
        first_at = (1 - c) * x + c * y
        second_at = (1 - c) * y + c * x

        def step_id(first, d):
            dx = (1 - c) * d if first else c * d
            dy = d - dx
            return device((y + dy) % 4, zh, zl, (x + dx) % 4, c)

        copies = [
            send(
                gsend.at[w, (first_at + d) % 4], grecv.at[w, d - 1], xss.at[w, d - 1], xrs.at[w, d - 1],
                step_id(True, d),
            )
            for d in (2, 1, 3)
        ]
        yield
        arrived(copies)

        def first_sum(k):
            total = gsend[w, first_at, k].astype(F32)
            for d in range(3):
                total += grecv[w, d, k].astype(F32)
            return total.astype(BF)

        rest = first_sum(8)
        for k in range(4):
            ysend[w, k, :, 0:128] = first_sum(2 * k)
            ysend[w, k, :, 128:256] = first_sum(2 * k + 1)
            ysend[w, k, :, 256:288] = rest[:, k * 32 : k * 32 + 32]
        copies = [
            send(
                ysend.at[w, (second_at + d) % 4], yrecv.at[w, d - 1], yss.at[w, d - 1], yrs.at[w, d - 1],
                step_id(False, d),
            )
            for d in (2, 1, 3)
        ]
        yield
        arrived(copies)
        total = ysend[w, second_at].astype(F32)
        for d in range(3):
            total += yrecv[w, d].astype(F32)
        for zh_ in range(4):
            for zl_ in range(4):
                chunk = total[zl_ * 18 : (zl_ + 1) * 18, zh_ * 72 : (zh_ + 1) * 72].astype(BF)
                zsend[w, zh_ * 4 + zl_, :, 0:72] = chunk[0:16]
                zsend[w, zh_ * 4 + zl_, 0:2, 72:108] = chunk[16:18, 0:36]
                zsend[w, zh_ * 4 + zl_, 2:4, 72:108] = chunk[16:18, 36:72]
        copies = [
            send(
                zsend.at[w, z_at[d - 1]], zrecv.at[w, d - 1], rss.at[w, d - 1], rrs.at[w, d - 1], z_ids[d - 1]
            )
            for d in (8, 7, 9, 6, 10, 5, 11, 4, 12, 3, 13, 2, 14, 1, 15)
        ]
        yield
        arrived(copies)
        total = zsend[w, zpos].astype(F32)
        for d in range(15):
            total += zrecv[w, d].astype(F32)
        sums[w] = total
        yield

    row = lax.broadcasted_iota(jnp.int32, (ROWS, ROWS), 0)
    col = lax.broadcasted_iota(jnp.int32, (ROWS, ROWS), 1)
    same_frame = (row // 64) == (col // 64)
    same_patch = (row % 8) == (col % 8)

    loads["cot"].wait()
    to_peers(cot[...].astype(F32), cot_s)
    loads["sqkv"].wait()

    attend(sqkv, same_frame, ps_ref, so, range(8))
    loads["wos"].wait()
    loads["tok"].wait()
    loads["pick"].wait()
    loads["wot"].wait()
    hidden = tok[...].astype(F32) + nn(so[...], wos[...])
    hid[...] = hidden.astype(BF)
    to_peers(so[...].astype(F32), so_s)
    to_peers(hidden, hid_s)

    own.wait()
    pl.semaphore_wait(barrier, len(everyone))
    hidden_copies = exchange(0, hid_s, hid_r)
    steps = gather()
    next(steps)
    next(steps)
    cot_copies = exchange(1, cot_s, cot_r)
    spatial_copies = exchange(4, so_s, so_r)
    arrived(hidden_copies)

    def shard_of(s, y_):
        upper = wbuf[s, 0, :, y_].reshape(HD, 128)
        lower = wbuf[s, 1, y_].reshape(HD, 128)
        return jnp.concatenate([upper, lower], axis=0)

    def project(i):
        rows = hid_r[...].reshape(ROWS, D)
        for pair in range(2):
            both = jnp.concatenate([shard_of(zsets[i], 2 * pair), shard_of(zsets[i], 2 * pair + 1)], axis=1)
            out = nn(rows, both).astype(BF)
            for k in range(2):
                tqkvp[(2 * pair + k) * 4 + zsets[i]] = out[:, k * 128 : (k + 1) * 128]

    for i in range(4):
        next(steps)
        project(i)
    for s in range(16):
        tqkv[:, s * COLS : (s + 1) * COLS] = tqkvp[s, :, 0:COLS]

    arrived(cot_copies)
    cot_swap = send(cot_r, cotx, oss.at[2], ors.at[2], partner)
    attend(tqkv, same_patch, pt_ref, to, range(8))
    to_s[...] = to[...].reshape(8, 16, HD)
    out_copies = exchange(2, to_s, to_r)
    temporal_left = left_operand(1, to[...])
    og[...] = nt(cot_r[...].reshape(ROWS, D), wot[...]).astype(BF)
    arrived(spatial_copies)
    spatial_left = left_operand(0, so_r[...].reshape(ROWS, HD))
    def temporal_product(part, xk):
        mine = nn(lt[1, c, part], cot_r[...].reshape(ROWS, D))
        return mine + nn(ltx[1, part], cotx[...].reshape(ROWS, D))

    def spatial_product(part, xk):
        mine = nn(lt[0, c, part], tg_s[...].reshape(ROWS, D))
        return mine + nn(ltx[0, part], tgx[...].reshape(ROWS, D))

    temporal_sum = weight_sum(1, temporal_product)
    spatial_sum = weight_sum(0, spatial_product)
    arrived((temporal_left, cot_swap))
    next(temporal_sum)
    next(temporal_sum)
    attend_grad(tqkv, pt_ref, og, dqkv, range(8))

    total = None
    for pair in range(8):
        grads, weights = [], []
        for k in range(2):
            s = 2 * pair + k
            grads += [dqkv[:, s * COLS : (s + 1) * COLS], jnp.zeros((ROWS, 128 - COLS), BF)]
            weights.append(shard_of(s % 4, s // 4))
        part = nt(jnp.concatenate(grads, axis=1), jnp.concatenate(weights, axis=1))
        total = part if total is None else total + part
    total = cot_r[...].reshape(ROWS, D).astype(F32) + total.astype(BF).astype(F32)
    tg_s[...] = total.astype(BF).reshape(8, 16, D)
    tg_swap = send(tg_s, tgx, oss.at[3], ors.at[3], partner)
    tokens_copies = exchange(3, tg_s, tg_r)
    next(temporal_sum)
    arrived((tg_swap, spatial_left))
    next(spatial_sum)
    next(spatial_sum)

    arrived(out_copies)
    block[...] = (hid[...].astype(F32) + nn(from_peers(to_r).astype(BF), wot[...])).astype(BF)
    outs = [pltpu.make_async_copy(block, block_hbm, out_sems.at[0])]
    outs[0].start()
    next(temporal_sum)
    arrived(tokens_copies)
    tgrad[...] = from_peers(tg_r).astype(BF)
    outs.append(pltpu.make_async_copy(tgrad, tgrad_hbm, out_sems.at[1]))
    outs[1].start()
    sog[...] = nt(tgrad[...], wos[...]).astype(BF)
    next(spatial_sum)
    attend_grad(sqkv, ps_ref, sog, sgrad, range(0, 4))
    next(spatial_sum)
    attend_grad(sqkv, ps_ref, sog, sgrad, range(4, 8))
    outs.append(pltpu.make_async_copy(sgrad, sgrad_hbm, out_sems.at[2]))
    outs[2].start()
    next(temporal_sum)
    next(spatial_sum)
    outs.append(pltpu.make_async_copy(sums, sums_hbm, out_sems.at[3]))
    outs[3].start()
    for copy in outs:
        copy.wait()
    for copy in pending:
        copy.wait_send()


def finish_kernel(
    block_hbm, tgrad_hbm, sgrad_hbm, sums_hbm, o1, o2, o3, o4, o5, block, tgrad, sgrad, sums, s1, s2, in_sems, out_sems
):
    ins = [
        pltpu.make_async_copy(src, dst, in_sems.at[n])
        for n, (src, dst) in enumerate(
            ((sums_hbm, sums), (block_hbm, block), (tgrad_hbm, tgrad), (sgrad_hbm, sgrad))
        )
    ]
    for copy in ins:
        copy.start()
    ins[0].wait()
    for n, out in enumerate((s1, s2)):
        out[0:16] = sums[n, :, 0:72]
        out[16:18, 0:36] = sums[n, 0:2, 72:108]
        out[16:18, 36:72] = sums[n, 2:4, 72:108]
    outs = []
    for n, (src, dst) in enumerate(((s1, o4), (s2, o5), (block, o1), (tgrad, o2), (sgrad, o3))):
        if n >= 2:
            ins[n - 1].wait()
        outs.append(pltpu.make_async_copy(src, dst, out_sems.at[n]))
        outs[-1].start()
    for copy in outs:
        copy.wait()


def picker():
    pick = np.zeros((2, 4, 80, HD), np.float32)
    for zl in range(4):
        for x in range(4):
            for core in range(2):
                for i in range(18):
                    pick[core, x, zl * 18 + i, ((zl * 4 + x) * 2 + core) * 18 + i] = 1
    return jnp.asarray(pick.reshape(640, HD), BF)


def shards(tokens, spatial_qkv, wo_spatial, w_temporal, wo_temporal, cotangent):
    frames, patches, _ = tokens.shape
    sems = pltpu.SemaphoreType.DMA

    def vm(*shape, dtype=BF):
        return pltpu.VMEM(shape, dtype)

    scratch = [
        vm(ROWS, D), vm(ROWS, 3 * HD), vm(HD, D), vm(COLS, D), vm(D, 128), vm(HD, D), vm(ROWS, D),
        vm(640, HD), vm(4, 2, 4, 4, 144, 128),
        vm(ROWS, D), vm(8, 16, D), vm(8, 16, D), vm(8, 16, D), vm(8, 16, D),
        vm(8, 16, D), vm(8, 16, D), vm(8, 16, HD), vm(8, 16, HD),
        vm(8, ROWS, ROWS, dtype=F32), vm(8, ROWS, ROWS, dtype=F32),
        vm(ROWS, HD), vm(ROWS, 3 * HD), vm(16, ROWS, 128), vm(ROWS, HD), vm(ROWS, HD),
        vm(ROWS, 3 * HD), vm(ROWS, D), vm(ROWS, HD), vm(ROWS, 3 * HD), vm(ROWS, D),
        vm(8, 16, HD), vm(8, 16, HD), vm(8, 16, D), vm(8, 16, D),
        vm(2, 2, 320, ROWS), vm(2, 320, ROWS),
        vm(2, 4, 9, 80, 128), vm(2, 3, 9, 80, 128), vm(2, 4, 80, 384), vm(2, 3, 80, 384),
        vm(2, 16, 16, 128), vm(2, 15, 16, 128), vm(2, 16, 128, dtype=F32),
        sems((7,)), sems((4,)), sems,
        sems((4,)), sems((4,)), sems((4, 4)), sems((4, 4)), sems((4, 4)), sems((4, 4)),
        sems((4, 4)), sems((4, 4)), sems((5, 7)), sems((5, 7)), sems((4,)), sems((4,)),
        sems((2, 3)), sems((2, 3)), sems((2, 3)), sems((2, 3)), sems((2, 15)), sems((2, 15)),
    ]
    anywhere = pl.BlockSpec(memory_space=pl.ANY)
    block_out, tokens_grad, qkv_grad, sums = pl.pallas_call(
        kernel,
        out_shape=[
            jax.ShapeDtypeStruct((ROWS, D), BF), jax.ShapeDtypeStruct((ROWS, D), BF),
            jax.ShapeDtypeStruct((ROWS, 3 * HD), BF), jax.ShapeDtypeStruct((2, 16, 128), F32),
        ],
        in_specs=[anywhere] * 7,
        out_specs=[anywhere] * 4,
        scratch_shapes=scratch,
        compiler_params=pltpu.CompilerParams(
            collective_id=0, has_side_effects=True, vmem_limit_bytes=62 * 1024 * 1024
        ),
        name="block",
    )(
        tokens.reshape(ROWS, D), spatial_qkv.reshape(ROWS, 3 * HD), wo_spatial, w_temporal.T,
        wo_temporal, cotangent.reshape(ROWS, D), picker(),
    )
    block_out, tokens_grad, qkv_grad, spatial_sum, temporal_sum = pl.pallas_call(
        finish_kernel,
        out_shape=[
            jax.ShapeDtypeStruct((ROWS, D), BF), jax.ShapeDtypeStruct((ROWS, D), BF),
            jax.ShapeDtypeStruct((ROWS, 3 * HD), BF),
            jax.ShapeDtypeStruct((18, 72), F32), jax.ShapeDtypeStruct((18, 72), F32),
        ],
        in_specs=[anywhere] * 4,
        out_specs=[anywhere] * 5,
        scratch_shapes=[
            vm(ROWS, D), vm(ROWS, D), vm(ROWS, 3 * HD), vm(2, 16, 128, dtype=F32),
            vm(18, 72, dtype=F32), vm(18, 72, dtype=F32), sems((4,)), sems((5,)),
        ],
        name="finish",
    )(block_out, tokens_grad, qkv_grad, sums)
    return (
        block_out.reshape(frames, patches, D),
        tokens_grad.reshape(frames, patches, D),
        qkv_grad.reshape(frames, patches, 3 * HD),
        spatial_sum,
        temporal_sum,
    )


def solution(mesh):
    rows = P(("dp", "seq"), None, None)
    return jax.shard_map(
        shards,
        mesh=mesh,
        in_specs=(rows, rows, P(), P(None, "dp"), P(), rows),
        out_specs=(rows, rows, rows, P("seq", "dp"), P("seq", "dp")),
        check_vma=False,
    )
```

```python
import functools
import math

import jax
import jax.numpy as jnp
import numpy as np
from jax import lax
from jax.experimental import pallas as pl
from jax.experimental.pallas import tpu as pltpu
from jax.sharding import PartitionSpec as P

DH = 72
HEADS = 8
HD = 576
D = 1152
ROWS = 128
COLS = 108
SCALE = 1.0 / math.sqrt(DH)
MESH = pl.DeviceIdType.MESH
BF = jnp.bfloat16
F32 = jnp.float32


def device(y, zh, zl, x, core):
    return (y * 4 + zh, (zl * 4 + x) * 2 + core)


def nt(left, right):
    return lax.dot_general(left, right, (((1,), (1,)), ((), ())), preferred_element_type=F32)


def tn(left, right):
    return lax.dot_general(left, right, (((0,), (0,)), ((), ())), preferred_element_type=F32)


def nn(left, right):
    return jnp.dot(left, right, preferred_element_type=F32)


def head(ref, n):
    return ref[:, n * DH : (n + 1) * DH]


def attend(qkv_ref, mask, p_ref, out_ref, heads):
    for h in heads:
        scores = nt(head(qkv_ref, h), head(qkv_ref, HEADS + h)) * SCALE
        scores = jnp.where(mask, scores, -1e30)
        scores = jnp.exp(scores - jnp.max(scores, axis=-1, keepdims=True))
        weights = scores / jnp.sum(scores, axis=-1, keepdims=True)
        p_ref[h] = weights
        out = nn(weights.astype(BF), head(qkv_ref, 2 * HEADS + h))
        out_ref[:, h * DH : (h + 1) * DH] = out.astype(BF)


def attend_grad(qkv_ref, p_ref, g_ref, grad_ref, heads):
    for h in heads:
        weights = p_ref[h]
        grad = head(g_ref, h)
        value_grad = tn(weights.astype(BF), grad)
        weight_grad = nt(grad, head(qkv_ref, 2 * HEADS + h))
        centered = weight_grad - jnp.sum(weights * weight_grad, axis=-1, keepdims=True)
        score_grad = (weights * centered * SCALE).astype(BF)
        query_grad = nn(score_grad, head(qkv_ref, HEADS + h))
        key_grad = tn(score_grad, head(qkv_ref, h))
        for part, value in enumerate((query_grad, key_grad, value_grad)):
            at = (part * HEADS + h) * DH
            grad_ref[:, at : at + DH] = value.astype(BF)


def to_peers(value, send_ref):
    for j in range(8):
        block = jnp.concatenate([value[8 * j : 8 * j + 8], value[64 + 8 * j : 72 + 8 * j]], axis=0)
        send_ref[j] = block.astype(BF)


def from_peers(recv_ref):
    blocks = [recv_ref[j].astype(F32) for j in range(8)]
    return jnp.concatenate([b[:8] for b in blocks] + [b[8:] for b in blocks], axis=0)


def kernel(
    tokens_hbm, sqkv_hbm, wos_hbm, w_hbm, wot_hbm, cot_hbm, pick_hbm,
    block_hbm, tgrad_hbm, sgrad_hbm, sums_hbm,
    tok, sqkv, wos, wraw, wpad, wot, cot, pick, wbuf,
    hid, hid_s, hid_r, cot_s, cot_r, tg_s, tg_r, to_s, to_r,
    ps_ref, pt_ref, so, tqkv, tqkvp, to, og, dqkv, tgrad, sog, sgrad, block,
    so_s, so_r, cotx, tgx, lt, ltx, gsend, grecv, ysend, yrecv, zsend, zrecv, sums,
    load_sems, out_sems, own_sem,
    zss, zrs, fss, frs, sss, srs, css, crs, ass, ars, oss, ors, xss, xrs, yss, yrs, rss, rrs,
):
    dp, seq = lax.axis_index("dp"), lax.axis_index("seq")
    y, zh, zl, x, c = dp // 4, dp % 4, seq // 8, (seq // 2) % 4, seq % 2
    u = (1 - c) * y + c * x
    v = (1 - c) * x + c * y
    zpos = zh * 4 + zl

    def at(u_, v_):
        return device((1 - c) * u_ + c * v_, zh, zl, (1 - c) * v_ + c * u_, c)

    partner = device(y, zh, zl, x, 1 - c)
    me = x * 2 + c
    peers = [(me + d) % 8 for d in range(1, 8)]
    peer_ids = [device(y, zh, zl, j // 2, j % 2) for j in peers]
    y_ids = [device((y + d) % 4, zh, zl, x, c) for d in range(1, 4)]
    x_ids = [device(y, zh, zl, (x + d) % 4, c) for d in range(1, 4)]
    z_at = [(zpos + d) % 16 for d in range(1, 16)]
    z_ids = [device(y, z // 4, z % 4, x, c) for z in z_at]
    everyone = peer_ids + y_ids + z_ids

    barrier = pltpu.get_barrier_semaphore()
    for target in everyone:
        pl.semaphore_signal(barrier, inc=1, device_id=target, device_id_type=MESH)

    loads = {}
    for n, (name, src, dst) in enumerate(
        (
            ("w", w_hbm, wraw), ("sqkv", sqkv_hbm, sqkv), ("cot", cot_hbm, cot), ("wot", wot_hbm, wot),
            ("wos", wos_hbm, wos), ("tok", tokens_hbm, tok), ("pick", pick_hbm, pick),
        )
    ):
        loads[name] = pltpu.make_async_copy(src, dst, load_sems.at[n])
        loads[name].start()
    pending = []

    def send(src, dst, send_sem, recv_sem, target):
        copy = pltpu.make_async_remote_copy(
            src_ref=src, dst_ref=dst, send_sem=send_sem, recv_sem=recv_sem,
            device_id=target, device_id_type=MESH,
        )
        copy.start()
        pending.append(copy)
        return copy

    loads["w"].wait()
    turned = wraw[...].astype(F32).T.astype(BF)
    wpad[...] = jnp.concatenate([turned, jnp.zeros((D, 128 - COLS), BF)], axis=1)
    own = pltpu.make_async_copy(wpad.at[pl.ds((c * 4 + x) * 144, 144)], wbuf.at[zh, c, v, u], own_sem)
    own.start()

    def ring(slot, low, high, pos, ids, ss, rs):
        state = {}

        def start():
            ref = slot(pos)
            state["up"] = send(ref, ref, ss.at[0], rs.at[0], ids[0])
            state["down"] = send(ref, ref, ss.at[1], rs.at[1], ids[2])

        def relay():
            state["up"].wait_recv()
            ref = low(slot((pos + 3) % 4))
            state["up2"] = send(ref, ref, ss.at[2], rs.at[2], ids[0])
            state["down"].wait_recv()
            ref = high(slot((pos + 1) % 4))
            state["down2"] = send(ref, ref, ss.at[3], rs.at[3], ids[2])

        def finish():
            state["up2"].wait_recv()
            state["down2"].wait_recv()

        return start, relay, finish

    def direct(slot, pos, ids, ss, rs):
        state = {}

        def start():
            ref = slot(pos)
            for d in (2, 1, 3):
                state[d] = send(ref, ref, ss.at[d - 1], rs.at[d - 1], ids[d - 1])

        def near():
            state[1].wait_recv()
            state[3].wait_recv()

        def far():
            state[2].wait_recv()

        return start, near, far

    zring_ids = [device(y, (zh + d) % 4, zl, x, c) for d in range(1, 4)]
    u_ids = [at((u + d) % 4, v) for d in range(1, 4)]
    v_ids = [at(u, (v + d) % 4) for d in range(1, 4)]
    zr = direct(lambda p: wbuf.at[p, c, v, u], zh, zring_ids, zss, zrs)
    order = (0, 1, 3, 2)
    zsets = [(zh + 4 - e) % 4 for e in order]
    fr = [
        direct(lambda p, s=s: wbuf.at[s, c, v, p], u, u_ids, fss.at[i], frs.at[i])
        for i, s in enumerate(zsets)
    ]
    sr = [
        ring(
            lambda p, s=s: wbuf.at[s, c, p], lambda r: r.at[pl.ds(0, 2)], lambda r: r.at[pl.ds(2, 2)],
            v, v_ids, sss.at[i], srs.at[i],
        )
        for i, s in enumerate(zsets)
    ]

    crosses = {}

    def cross(i, d):
        ref = wbuf.at[zsets[i], c, (v + d) % 4]
        crosses[i, d] = send(ref, ref, css.at[i, d], crs.at[i, d], partner)

    def stage_c(i):
        fr[i][1]()
        fr[i][2]()
        sr[i][0]()
        cross(i, 0)

    def stage_d(i):
        sr[i][1]()
        cross(i, 3)
        cross(i, 1)

    def stage_e(i):
        sr[i][2]()
        cross(i, 2)

    def stage_f(i):
        for d in range(4):
            crosses[i, d].wait_recv()

    def gather():
        zr[0]()
        fr[0][0]()
        stage_c(0)
        zr[1]()
        fr[1][0]()
        fr[2][0]()
        stage_d(0)
        zr[2]()
        fr[3][0]()
        stage_c(1)
        stage_c(2)
        yield
        stage_e(0)
        stage_c(3)
        stage_d(1)
        stage_d(2)
        stage_d(3)
        yield
        stage_f(0)
        yield
        stage_e(1)
        stage_e(2)
        stage_f(1)
        yield
        stage_f(2)
        yield
        stage_e(3)
        stage_f(3)
        yield

    def exchange(n, src, dst):
        copies = []
        for d in (4, 3, 5, 2, 6, 1, 7):
            copies.append(
                send(src.at[peers[d - 1]], dst.at[me], ass.at[n, d - 1], ars.at[n, d - 1], peer_ids[d - 1])
            )
        dst[me] = src[me]
        return copies

    def arrived(copies):
        for copy in copies:
            copy.wait_recv()

    def left_operand(n, value):
        lt[n] = nt(pick[...], value).astype(BF).reshape(2, 320, ROWS)
        return send(lt.at[n, 1 - c], ltx.at[n], oss.at[n], ors.at[n], partner)

    def weight_sum(w, product):
        for xk in range(4):
            total = product(pl.ds(xk * 80, 80), xk)
            for yk in range(4):
                first, second = (1 - c) * xk + c * yk, (1 - c) * yk + c * xk
                for k in range(2):
                    at_ = yk * 288 + k * 128
                    gsend[w, first, 2 * second + k] = total[:, at_ : at_ + 128].astype(BF)
            rests = [total[:, yk * 288 + 256 : yk * 288 + 288].astype(BF) for yk in range(4)]

            @pl.when(c == 0)
            def _():
                for yk in range(4):
                    gsend[w, xk, 8, :, yk * 32 : yk * 32 + 32] = rests[yk]

            @pl.when(c == 1)
            def _():
                for yk in range(4):
                    gsend[w, yk, 8, :, xk * 32 : xk * 32 + 32] = rests[yk]

        yield
        first_at = (1 - c) * x + c * y
        second_at = (1 - c) * y + c * x

        def step_id(first, d):
            dx = (1 - c) * d if first else c * d
            dy = d - dx
            return device((y + dy) % 4, zh, zl, (x + dx) % 4, c)

        copies = [
            send(
                gsend.at[w, (first_at + d) % 4], grecv.at[w, d - 1], xss.at[w, d - 1], xrs.at[w, d - 1],
                step_id(True, d),
            )
            for d in (2, 1, 3)
        ]
        yield
        arrived(copies)

        def first_sum(k):
            total = gsend[w, first_at, k].astype(F32)
            for d in range(3):
                total += grecv[w, d, k].astype(F32)
            return total.astype(BF)

        rest = first_sum(8)
        for k in range(4):
            ysend[w, k, :, 0:128] = first_sum(2 * k)
            ysend[w, k, :, 128:256] = first_sum(2 * k + 1)
            ysend[w, k, :, 256:288] = rest[:, k * 32 : k * 32 + 32]
        copies = [
            send(
                ysend.at[w, (second_at + d) % 4], yrecv.at[w, d - 1], yss.at[w, d - 1], yrs.at[w, d - 1],
                step_id(False, d),
            )
            for d in (2, 1, 3)
        ]
        yield
        arrived(copies)
        total = ysend[w, second_at].astype(F32)
        for d in range(3):
            total += yrecv[w, d].astype(F32)
        for zh_ in range(4):
            for zl_ in range(4):
                chunk = total[zl_ * 18 : (zl_ + 1) * 18, zh_ * 72 : (zh_ + 1) * 72].astype(BF)
                zsend[w, zh_ * 4 + zl_, :, 0:72] = chunk[0:16]
                zsend[w, zh_ * 4 + zl_, 0:2, 72:108] = chunk[16:18, 0:36]
                zsend[w, zh_ * 4 + zl_, 2:4, 72:108] = chunk[16:18, 36:72]
        copies = [
            send(
                zsend.at[w, z_at[d - 1]], zrecv.at[w, d - 1], rss.at[w, d - 1], rrs.at[w, d - 1], z_ids[d - 1]
            )
            for d in (8, 7, 9, 6, 10, 5, 11, 4, 12, 3, 13, 2, 14, 1, 15)
        ]
        yield
        arrived(copies)
        total = zsend[w, zpos].astype(F32)
        for d in range(15):
            total += zrecv[w, d].astype(F32)
        sums[w] = total
        yield

    row = lax.broadcasted_iota(jnp.int32, (ROWS, ROWS), 0)
    col = lax.broadcasted_iota(jnp.int32, (ROWS, ROWS), 1)
    same_frame = (row // 64) == (col // 64)
    same_patch = (row % 8) == (col % 8)

    loads["cot"].wait()
    to_peers(cot[...].astype(F32), cot_s)
    loads["sqkv"].wait()

    attend(sqkv, same_frame, ps_ref, so, range(8))
    loads["wos"].wait()
    loads["tok"].wait()
    loads["pick"].wait()
    loads["wot"].wait()
    hidden = tok[...].astype(F32) + nn(so[...], wos[...])
    hid[...] = hidden.astype(BF)
    to_peers(so[...].astype(F32), so_s)
    to_peers(hidden, hid_s)

    own.wait()
    pl.semaphore_wait(barrier, len(everyone))
    hidden_copies = exchange(0, hid_s, hid_r)
    steps = gather()
    next(steps)
    next(steps)
    cot_copies = exchange(1, cot_s, cot_r)
    spatial_copies = exchange(4, so_s, so_r)
    arrived(hidden_copies)

    def shard_of(s, y_):
        upper = wbuf[s, 0, :, y_].reshape(HD, 128)
        lower = wbuf[s, 1, y_].reshape(HD, 128)
        return jnp.concatenate([upper, lower], axis=0)

    def project(i):
        rows = hid_r[...].reshape(ROWS, D)
        for pair in range(2):
            both = jnp.concatenate([shard_of(zsets[i], 2 * pair), shard_of(zsets[i], 2 * pair + 1)], axis=1)
            out = nn(rows, both).astype(BF)
            for k in range(2):
                tqkvp[(2 * pair + k) * 4 + zsets[i]] = out[:, k * 128 : (k + 1) * 128]

    for i in range(4):
        next(steps)
        project(i)
    for s in range(16):
        tqkv[:, s * COLS : (s + 1) * COLS] = tqkvp[s, :, 0:COLS]

    arrived(cot_copies)
    cot_swap = send(cot_r, cotx, oss.at[2], ors.at[2], partner)
    attend(tqkv, same_patch, pt_ref, to, range(8))
    to_s[...] = to[...].reshape(8, 16, HD)
    out_copies = exchange(2, to_s, to_r)
    temporal_left = left_operand(1, to[...])
    og[...] = nt(cot_r[...].reshape(ROWS, D), wot[...]).astype(BF)
    arrived(spatial_copies)
    spatial_left = left_operand(0, so_r[...].reshape(ROWS, HD))
    def temporal_product(part, xk):
        mine = nn(lt[1, c, part], cot_r[...].reshape(ROWS, D))
        return mine + nn(ltx[1, part], cotx[...].reshape(ROWS, D))

    def spatial_product(part, xk):
        mine = nn(lt[0, c, part], tg_s[...].reshape(ROWS, D))
        return mine + nn(ltx[0, part], tgx[...].reshape(ROWS, D))

    temporal_sum = weight_sum(1, temporal_product)
    spatial_sum = weight_sum(0, spatial_product)
    arrived((temporal_left, cot_swap))
    next(temporal_sum)
    next(temporal_sum)
    attend_grad(tqkv, pt_ref, og, dqkv, range(8))

    total = None
    for pair in range(8):
        grads, weights = [], []
        for k in range(2):
            s = 2 * pair + k
            grads += [dqkv[:, s * COLS : (s + 1) * COLS], jnp.zeros((ROWS, 128 - COLS), BF)]
            weights.append(shard_of(s % 4, s // 4))
        part = nt(jnp.concatenate(grads, axis=1), jnp.concatenate(weights, axis=1))
        total = part if total is None else total + part
    total = cot_r[...].reshape(ROWS, D).astype(F32) + total.astype(BF).astype(F32)
    tg_s[...] = total.astype(BF).reshape(8, 16, D)
    tg_swap = send(tg_s, tgx, oss.at[3], ors.at[3], partner)
    tokens_copies = exchange(3, tg_s, tg_r)
    arrived((tg_swap, spatial_left))
    next(spatial_sum)
    next(spatial_sum)
    next(temporal_sum)

    arrived(out_copies)
    block[...] = (hid[...].astype(F32) + nn(from_peers(to_r).astype(BF), wot[...])).astype(BF)
    outs = [pltpu.make_async_copy(block, block_hbm, out_sems.at[0])]
    outs[0].start()
    next(temporal_sum)
    arrived(tokens_copies)
    tgrad[...] = from_peers(tg_r).astype(BF)
    outs.append(pltpu.make_async_copy(tgrad, tgrad_hbm, out_sems.at[1]))
    outs[1].start()
    sog[...] = nt(tgrad[...], wos[...]).astype(BF)
    next(spatial_sum)
    attend_grad(sqkv, ps_ref, sog, sgrad, range(0, 4))
    next(spatial_sum)
    attend_grad(sqkv, ps_ref, sog, sgrad, range(4, 8))
    outs.append(pltpu.make_async_copy(sgrad, sgrad_hbm, out_sems.at[2]))
    outs[2].start()
    next(temporal_sum)
    next(spatial_sum)
    outs.append(pltpu.make_async_copy(sums, sums_hbm, out_sems.at[3]))
    outs[3].start()
    for copy in outs:
        copy.wait()
    for copy in pending:
        copy.wait_send()


def finish_kernel(
    block_hbm, tgrad_hbm, sgrad_hbm, sums_hbm, o1, o2, o3, o4, o5, block, tgrad, sgrad, sums, s1, s2, in_sems, out_sems
):
    ins = [
        pltpu.make_async_copy(src, dst, in_sems.at[n])
        for n, (src, dst) in enumerate(
            ((sums_hbm, sums), (block_hbm, block), (tgrad_hbm, tgrad), (sgrad_hbm, sgrad))
        )
    ]
    for copy in ins:
        copy.start()
    ins[0].wait()
    for n, out in enumerate((s1, s2)):
        out[0:16] = sums[n, :, 0:72]
        out[16:18, 0:36] = sums[n, 0:2, 72:108]
        out[16:18, 36:72] = sums[n, 2:4, 72:108]
    outs = []
    for n, (src, dst) in enumerate(((s1, o4), (s2, o5), (block, o1), (tgrad, o2), (sgrad, o3))):
        if n >= 2:
            ins[n - 1].wait()
        outs.append(pltpu.make_async_copy(src, dst, out_sems.at[n]))
        outs[-1].start()
    for copy in outs:
        copy.wait()


def picker():
    pick = np.zeros((2, 4, 80, HD), np.float32)
    for zl in range(4):
        for x in range(4):
            for core in range(2):
                for i in range(18):
                    pick[core, x, zl * 18 + i, ((zl * 4 + x) * 2 + core) * 18 + i] = 1
    return jnp.asarray(pick.reshape(640, HD), BF)


def shards(tokens, spatial_qkv, wo_spatial, w_temporal, wo_temporal, cotangent):
    frames, patches, _ = tokens.shape
    sems = pltpu.SemaphoreType.DMA

    def vm(*shape, dtype=BF):
        return pltpu.VMEM(shape, dtype)

    scratch = [
        vm(ROWS, D), vm(ROWS, 3 * HD), vm(HD, D), vm(COLS, D), vm(D, 128), vm(HD, D), vm(ROWS, D),
        vm(640, HD), vm(4, 2, 4, 4, 144, 128),
        vm(ROWS, D), vm(8, 16, D), vm(8, 16, D), vm(8, 16, D), vm(8, 16, D),
        vm(8, 16, D), vm(8, 16, D), vm(8, 16, HD), vm(8, 16, HD),
        vm(8, ROWS, ROWS, dtype=F32), vm(8, ROWS, ROWS, dtype=F32),
        vm(ROWS, HD), vm(ROWS, 3 * HD), vm(16, ROWS, 128), vm(ROWS, HD), vm(ROWS, HD),
        vm(ROWS, 3 * HD), vm(ROWS, D), vm(ROWS, HD), vm(ROWS, 3 * HD), vm(ROWS, D),
        vm(8, 16, HD), vm(8, 16, HD), vm(8, 16, D), vm(8, 16, D),
        vm(2, 2, 320, ROWS), vm(2, 320, ROWS),
        vm(2, 4, 9, 80, 128), vm(2, 3, 9, 80, 128), vm(2, 4, 80, 384), vm(2, 3, 80, 384),
        vm(2, 16, 16, 128), vm(2, 15, 16, 128), vm(2, 16, 128, dtype=F32),
        sems((7,)), sems((4,)), sems,
        sems((4,)), sems((4,)), sems((4, 4)), sems((4, 4)), sems((4, 4)), sems((4, 4)),
        sems((4, 4)), sems((4, 4)), sems((5, 7)), sems((5, 7)), sems((4,)), sems((4,)),
        sems((2, 3)), sems((2, 3)), sems((2, 3)), sems((2, 3)), sems((2, 15)), sems((2, 15)),
    ]
    anywhere = pl.BlockSpec(memory_space=pl.ANY)
    block_out, tokens_grad, qkv_grad, sums = pl.pallas_call(
        kernel,
        out_shape=[
            jax.ShapeDtypeStruct((ROWS, D), BF), jax.ShapeDtypeStruct((ROWS, D), BF),
            jax.ShapeDtypeStruct((ROWS, 3 * HD), BF), jax.ShapeDtypeStruct((2, 16, 128), F32),
        ],
        in_specs=[anywhere] * 7,
        out_specs=[anywhere] * 4,
        scratch_shapes=scratch,
        compiler_params=pltpu.CompilerParams(
            collective_id=0, has_side_effects=True, vmem_limit_bytes=62 * 1024 * 1024
        ),
        name="block",
    )(
        tokens.reshape(ROWS, D), spatial_qkv.reshape(ROWS, 3 * HD), wo_spatial, w_temporal.T,
        wo_temporal, cotangent.reshape(ROWS, D), picker(),
    )
    block_out, tokens_grad, qkv_grad, spatial_sum, temporal_sum = pl.pallas_call(
        finish_kernel,
        out_shape=[
            jax.ShapeDtypeStruct((ROWS, D), BF), jax.ShapeDtypeStruct((ROWS, D), BF),
            jax.ShapeDtypeStruct((ROWS, 3 * HD), BF),
            jax.ShapeDtypeStruct((18, 72), F32), jax.ShapeDtypeStruct((18, 72), F32),
        ],
        in_specs=[anywhere] * 4,
        out_specs=[anywhere] * 5,
        scratch_shapes=[
            vm(ROWS, D), vm(ROWS, D), vm(ROWS, 3 * HD), vm(2, 16, 128, dtype=F32),
            vm(18, 72, dtype=F32), vm(18, 72, dtype=F32), sems((4,)), sems((5,)),
        ],
        name="finish",
    )(block_out, tokens_grad, qkv_grad, sums)
    return (
        block_out.reshape(frames, patches, D),
        tokens_grad.reshape(frames, patches, D),
        qkv_grad.reshape(frames, patches, 3 * HD),
        spatial_sum,
        temporal_sum,
    )


def solution(mesh):
    rows = P(("dp", "seq"), None, None)
    return jax.shard_map(
        shards,
        mesh=mesh,
        in_specs=(rows, rows, P(), P(None, "dp"), P(), rows),
        out_specs=(rows, rows, rows, P("seq", "dp"), P("seq", "dp")),
        check_vma=False,
    )
```

```python
import functools
import math

import jax
import jax.numpy as jnp
import numpy as np
from jax import lax
from jax.experimental import pallas as pl
from jax.experimental.pallas import tpu as pltpu
from jax.sharding import PartitionSpec as P

DH = 72
HEADS = 8
HD = 576
D = 1152
ROWS = 128
COLS = 108
SCALE = 1.0 / math.sqrt(DH)
MESH = pl.DeviceIdType.MESH
BF = jnp.bfloat16
F32 = jnp.float32


def device(y, zh, zl, x, core):
    return (y * 4 + zh, (zl * 4 + x) * 2 + core)


def nt(left, right):
    return lax.dot_general(left, right, (((1,), (1,)), ((), ())), preferred_element_type=F32)


def tn(left, right):
    return lax.dot_general(left, right, (((0,), (0,)), ((), ())), preferred_element_type=F32)


def nn(left, right):
    return jnp.dot(left, right, preferred_element_type=F32)


def head(ref, n):
    return ref[:, n * DH : (n + 1) * DH]


def attend(qkv_ref, mask, p_ref, out_ref, heads):
    for h in heads:
        scores = nt(head(qkv_ref, h), head(qkv_ref, HEADS + h)) * SCALE
        scores = jnp.where(mask, scores, -1e30)
        scores = jnp.exp(scores - jnp.max(scores, axis=-1, keepdims=True))
        weights = scores / jnp.sum(scores, axis=-1, keepdims=True)
        p_ref[h] = weights
        out = nn(weights.astype(BF), head(qkv_ref, 2 * HEADS + h))
        out_ref[:, h * DH : (h + 1) * DH] = out.astype(BF)


def attend_grad(qkv_ref, p_ref, g_ref, grad_ref, heads):
    for h in heads:
        weights = p_ref[h]
        grad = head(g_ref, h)
        value_grad = tn(weights.astype(BF), grad)
        weight_grad = nt(grad, head(qkv_ref, 2 * HEADS + h))
        centered = weight_grad - jnp.sum(weights * weight_grad, axis=-1, keepdims=True)
        score_grad = (weights * centered * SCALE).astype(BF)
        query_grad = nn(score_grad, head(qkv_ref, HEADS + h))
        key_grad = tn(score_grad, head(qkv_ref, h))
        for part, value in enumerate((query_grad, key_grad, value_grad)):
            at = (part * HEADS + h) * DH
            grad_ref[:, at : at + DH] = value.astype(BF)


def to_peers(value, send_ref):
    for j in range(8):
        block = jnp.concatenate([value[8 * j : 8 * j + 8], value[64 + 8 * j : 72 + 8 * j]], axis=0)
        send_ref[j] = block.astype(BF)


def from_peers(recv_ref):
    blocks = [recv_ref[j].astype(F32) for j in range(8)]
    return jnp.concatenate([b[:8] for b in blocks] + [b[8:] for b in blocks], axis=0)


def kernel(
    tokens_hbm, sqkv_hbm, wos_hbm, w_hbm, wot_hbm, cot_hbm, pick_hbm,
    block_hbm, tgrad_hbm, sgrad_hbm, sums_hbm,
    tok, sqkv, wos, wraw, wpad, wot, cot, pick, wbuf,
    hid, hid_s, hid_r, cot_s, cot_r, tg_s, tg_r, to_s, to_r,
    ps_ref, pt_ref, so, tqkv, tqkvp, to, og, dqkv, tgrad, sog, sgrad, block,
    so_s, so_r, cotx, tgx, lt, ltx, gsend, grecv, ysend, yrecv, zsend, zrecv, sums,
    load_sems, out_sems, own_sem,
    zss, zrs, fss, frs, sss, srs, css, crs, ass, ars, oss, ors, xss, xrs, yss, yrs, rss, rrs,
):
    dp, seq = lax.axis_index("dp"), lax.axis_index("seq")
    y, zh, zl, x, c = dp // 4, dp % 4, seq // 8, (seq // 2) % 4, seq % 2
    u = (1 - c) * y + c * x
    v = (1 - c) * x + c * y
    zpos = zh * 4 + zl

    def at(u_, v_):
        return device((1 - c) * u_ + c * v_, zh, zl, (1 - c) * v_ + c * u_, c)

    partner = device(y, zh, zl, x, 1 - c)
    me = x * 2 + c
    peers = [(me + d) % 8 for d in range(1, 8)]
    peer_ids = [device(y, zh, zl, j // 2, j % 2) for j in peers]
    y_ids = [device((y + d) % 4, zh, zl, x, c) for d in range(1, 4)]
    x_ids = [device(y, zh, zl, (x + d) % 4, c) for d in range(1, 4)]
    z_at = [(zpos + d) % 16 for d in range(1, 16)]
    z_ids = [device(y, z // 4, z % 4, x, c) for z in z_at]
    everyone = peer_ids + y_ids + z_ids

    barrier = pltpu.get_barrier_semaphore()
    for target in everyone:
        pl.semaphore_signal(barrier, inc=1, device_id=target, device_id_type=MESH)

    loads = {}
    for n, (name, src, dst) in enumerate(
        (
            ("w", w_hbm, wraw), ("sqkv", sqkv_hbm, sqkv), ("cot", cot_hbm, cot), ("wot", wot_hbm, wot),
            ("wos", wos_hbm, wos), ("tok", tokens_hbm, tok), ("pick", pick_hbm, pick),
        )
    ):
        loads[name] = pltpu.make_async_copy(src, dst, load_sems.at[n])
        loads[name].start()
    pending = []

    def send(src, dst, send_sem, recv_sem, target):
        copy = pltpu.make_async_remote_copy(
            src_ref=src, dst_ref=dst, send_sem=send_sem, recv_sem=recv_sem,
            device_id=target, device_id_type=MESH,
        )
        copy.start()
        pending.append(copy)
        return copy

    loads["w"].wait()
    turned = wraw[...].astype(F32).T.astype(BF)
    wpad[...] = jnp.concatenate([turned, jnp.zeros((D, 128 - COLS), BF)], axis=1)
    own = pltpu.make_async_copy(wpad.at[pl.ds((c * 4 + x) * 144, 144)], wbuf.at[zh, c, v, u], own_sem)
    own.start()

    def ring(slot, low, high, pos, ids, ss, rs):
        state = {}

        def start():
            ref = slot(pos)
            state["up"] = send(ref, ref, ss.at[0], rs.at[0], ids[0])
            state["down"] = send(ref, ref, ss.at[1], rs.at[1], ids[2])

        def relay():
            state["up"].wait_recv()
            ref = low(slot((pos + 3) % 4))
            state["up2"] = send(ref, ref, ss.at[2], rs.at[2], ids[0])
            state["down"].wait_recv()
            ref = high(slot((pos + 1) % 4))
            state["down2"] = send(ref, ref, ss.at[3], rs.at[3], ids[2])

        def finish():
            state["up2"].wait_recv()
            state["down2"].wait_recv()

        return start, relay, finish

    def direct(slot, pos, ids, ss, rs):
        state = {}

        def start():
            ref = slot(pos)
            for d in (2, 1, 3):
                state[d] = send(ref, ref, ss.at[d - 1], rs.at[d - 1], ids[d - 1])

        def near():
            state[1].wait_recv()
            state[3].wait_recv()

        def far():
            state[2].wait_recv()

        return start, near, far

    zring_ids = [device(y, (zh + d) % 4, zl, x, c) for d in range(1, 4)]
    u_ids = [at((u + d) % 4, v) for d in range(1, 4)]
    v_ids = [at(u, (v + d) % 4) for d in range(1, 4)]
    zr = direct(lambda p: wbuf.at[p, c, v, u], zh, zring_ids, zss, zrs)
    order = (0, 1, 3, 2)
    zsets = [(zh + 4 - e) % 4 for e in order]
    fr = [
        direct(lambda p, s=s: wbuf.at[s, c, v, p], u, u_ids, fss.at[i], frs.at[i])
        for i, s in enumerate(zsets)
    ]
    sr = [
        ring(
            lambda p, s=s: wbuf.at[s, c, p], lambda r: r.at[pl.ds(0, 2)], lambda r: r.at[pl.ds(2, 2)],
            v, v_ids, sss.at[i], srs.at[i],
        )
        for i, s in enumerate(zsets)
    ]

    crosses = {}

    def cross(i, d):
        ref = wbuf.at[zsets[i], c, (v + d) % 4]
        crosses[i, d] = send(ref, ref, css.at[i, d], crs.at[i, d], partner)

    def stage_c(i):
        fr[i][1]()
        fr[i][2]()
        sr[i][0]()
        cross(i, 0)

    def stage_d(i):
        sr[i][1]()
        cross(i, 3)
        cross(i, 1)

    def stage_e(i):
        sr[i][2]()
        cross(i, 2)

    def stage_f(i):
        for d in range(4):
            crosses[i, d].wait_recv()

    def gather():
        zr[0]()
        fr[0][0]()
        stage_c(0)
        zr[1]()
        fr[1][0]()
        fr[2][0]()
        stage_d(0)
        zr[2]()
        fr[3][0]()
        stage_c(1)
        stage_c(2)
        yield
        stage_e(0)
        stage_c(3)
        stage_d(1)
        stage_d(2)
        stage_d(3)
        yield
        stage_f(0)
        yield
        stage_e(1)
        stage_e(2)
        stage_f(1)
        yield
        stage_f(2)
        yield
        stage_e(3)
        stage_f(3)
        yield

    def exchange(n, src, dst):
        copies = []
        for d in (4, 3, 5, 2, 6, 1, 7):
            copies.append(
                send(src.at[peers[d - 1]], dst.at[me], ass.at[n, d - 1], ars.at[n, d - 1], peer_ids[d - 1])
            )
        dst[me] = src[me]
        return copies

    def arrived(copies):
        for copy in copies:
            copy.wait_recv()

    def left_operand(n, value):
        lt[n] = nt(pick[...], value).astype(BF).reshape(2, 320, ROWS)
        return send(lt.at[n, 1 - c], ltx.at[n], oss.at[n], ors.at[n], partner)

    def weight_sum(w, product):
        for xk in range(4):
            total = product(pl.ds(xk * 80, 80), xk)
            for yk in range(4):
                first, second = (1 - c) * xk + c * yk, (1 - c) * yk + c * xk
                for k in range(2):
                    at_ = yk * 288 + k * 128
                    gsend[w, first, 2 * second + k] = total[:, at_ : at_ + 128].astype(BF)
            rests = [total[:, yk * 288 + 256 : yk * 288 + 288].astype(BF) for yk in range(4)]

            @pl.when(c == 0)
            def _():
                for yk in range(4):
                    gsend[w, xk, 8, :, yk * 32 : yk * 32 + 32] = rests[yk]

            @pl.when(c == 1)
            def _():
                for yk in range(4):
                    gsend[w, yk, 8, :, xk * 32 : xk * 32 + 32] = rests[yk]

        yield
        first_at = (1 - c) * x + c * y
        second_at = (1 - c) * y + c * x

        def step_id(first, d):
            dx = (1 - c) * d if first else c * d
            dy = d - dx
            return device((y + dy) % 4, zh, zl, (x + dx) % 4, c)

        copies = [
            send(
                gsend.at[w, (first_at + d) % 4], grecv.at[w, d - 1], xss.at[w, d - 1], xrs.at[w, d - 1],
                step_id(True, d),
            )
            for d in (2, 1, 3)
        ]
        yield
        arrived(copies)

        def first_sum(k):
            total = gsend[w, first_at, k].astype(F32)
            for d in range(3):
                total += grecv[w, d, k].astype(F32)
            return total.astype(BF)

        rest = first_sum(8)
        for k in range(4):
            ysend[w, k, :, 0:128] = first_sum(2 * k)
            ysend[w, k, :, 128:256] = first_sum(2 * k + 1)
            ysend[w, k, :, 256:288] = rest[:, k * 32 : k * 32 + 32]
        copies = [
            send(
                ysend.at[w, (second_at + d) % 4], yrecv.at[w, d - 1], yss.at[w, d - 1], yrs.at[w, d - 1],
                step_id(False, d),
            )
            for d in (2, 1, 3)
        ]
        yield
        arrived(copies)
        total = ysend[w, second_at].astype(F32)
        for d in range(3):
            total += yrecv[w, d].astype(F32)
        for zh_ in range(4):
            for zl_ in range(4):
                chunk = total[zl_ * 18 : (zl_ + 1) * 18, zh_ * 72 : (zh_ + 1) * 72].astype(BF)
                zsend[w, zh_ * 4 + zl_, :, 0:72] = chunk[0:16]
                zsend[w, zh_ * 4 + zl_, 0:2, 72:108] = chunk[16:18, 0:36]
                zsend[w, zh_ * 4 + zl_, 2:4, 72:108] = chunk[16:18, 36:72]
        copies = [
            send(
                zsend.at[w, z_at[d - 1]], zrecv.at[w, d - 1], rss.at[w, d - 1], rrs.at[w, d - 1], z_ids[d - 1]
            )
            for d in (8, 7, 9, 6, 10, 5, 11, 4, 12, 3, 13, 2, 14, 1, 15)
        ]
        yield
        arrived(copies)
        total = zsend[w, zpos].astype(F32)
        for d in range(15):
            total += zrecv[w, d].astype(F32)
        sums[w] = total
        yield

    row = lax.broadcasted_iota(jnp.int32, (ROWS, ROWS), 0)
    col = lax.broadcasted_iota(jnp.int32, (ROWS, ROWS), 1)
    same_frame = (row // 64) == (col // 64)
    same_patch = (row % 8) == (col % 8)

    loads["cot"].wait()
    to_peers(cot[...].astype(F32), cot_s)
    loads["sqkv"].wait()

    attend(sqkv, same_frame, ps_ref, so, range(8))
    loads["wos"].wait()
    loads["tok"].wait()
    loads["pick"].wait()
    loads["wot"].wait()
    hidden = tok[...].astype(F32) + nn(so[...], wos[...])
    hid[...] = hidden.astype(BF)
    to_peers(so[...].astype(F32), so_s)
    to_peers(hidden, hid_s)

    own.wait()
    pl.semaphore_wait(barrier, len(everyone))
    hidden_copies = exchange(0, hid_s, hid_r)
    steps = gather()
    next(steps)
    next(steps)
    cot_copies = exchange(1, cot_s, cot_r)
    spatial_copies = exchange(4, so_s, so_r)
    arrived(hidden_copies)

    def shard_of(s, y_):
        upper = wbuf[s, 0, :, y_].reshape(HD, 128)
        lower = wbuf[s, 1, y_].reshape(HD, 128)
        return jnp.concatenate([upper, lower], axis=0)

    def project(i):
        rows = hid_r[...].reshape(ROWS, D)
        for pair in range(2):
            both = jnp.concatenate([shard_of(zsets[i], 2 * pair), shard_of(zsets[i], 2 * pair + 1)], axis=1)
            out = nn(rows, both).astype(BF)
            for k in range(2):
                tqkvp[(2 * pair + k) * 4 + zsets[i]] = out[:, k * 128 : (k + 1) * 128]

    for i in range(4):
        next(steps)
        project(i)
    for s in range(16):
        tqkv[:, s * COLS : (s + 1) * COLS] = tqkvp[s, :, 0:COLS]

    arrived(cot_copies)
    cot_swap = send(cot_r, cotx, oss.at[2], ors.at[2], partner)
    attend(tqkv, same_patch, pt_ref, to, range(8))
    to_s[...] = to[...].reshape(8, 16, HD)
    temporal_left = left_operand(1, to[...])
    og[...] = nt(cot_r[...].reshape(ROWS, D), wot[...]).astype(BF)
    arrived(spatial_copies)
    spatial_left = left_operand(0, so_r[...].reshape(ROWS, HD))
    def temporal_product(part, xk):
        mine = nn(lt[1, c, part], cot_r[...].reshape(ROWS, D))
        return mine + nn(ltx[1, part], cotx[...].reshape(ROWS, D))

    def spatial_product(part, xk):
        mine = nn(lt[0, c, part], tg_s[...].reshape(ROWS, D))
        return mine + nn(ltx[0, part], tgx[...].reshape(ROWS, D))

    temporal_sum = weight_sum(1, temporal_product)
    spatial_sum = weight_sum(0, spatial_product)
    arrived((temporal_left, cot_swap))
    next(temporal_sum)
    next(temporal_sum)
    attend_grad(tqkv, pt_ref, og, dqkv, range(8))

    total = None
    for pair in range(8):
        grads, weights = [], []
        for k in range(2):
            s = 2 * pair + k
            grads += [dqkv[:, s * COLS : (s + 1) * COLS], jnp.zeros((ROWS, 128 - COLS), BF)]
            weights.append(shard_of(s % 4, s // 4))
        part = nt(jnp.concatenate(grads, axis=1), jnp.concatenate(weights, axis=1))
        total = part if total is None else total + part
    total = cot_r[...].reshape(ROWS, D).astype(F32) + total.astype(BF).astype(F32)
    tg_s[...] = total.astype(BF).reshape(8, 16, D)
    tg_swap = send(tg_s, tgx, oss.at[3], ors.at[3], partner)
    tokens_copies = exchange(3, tg_s, tg_r)
    arrived((tg_swap, spatial_left))
    next(spatial_sum)
    next(spatial_sum)
    out_copies = exchange(2, to_s, to_r)
    next(temporal_sum)

    outs = []
    next(temporal_sum)
    arrived(tokens_copies)
    tgrad[...] = from_peers(tg_r).astype(BF)
    outs.append(pltpu.make_async_copy(tgrad, tgrad_hbm, out_sems.at[1]))
    outs[0].start()
    sog[...] = nt(tgrad[...], wos[...]).astype(BF)
    next(spatial_sum)
    attend_grad(sqkv, ps_ref, sog, sgrad, range(0, 4))
    next(spatial_sum)
    attend_grad(sqkv, ps_ref, sog, sgrad, range(4, 8))
    outs.append(pltpu.make_async_copy(sgrad, sgrad_hbm, out_sems.at[2]))
    outs[1].start()
    arrived(out_copies)
    block[...] = (hid[...].astype(F32) + nn(from_peers(to_r).astype(BF), wot[...])).astype(BF)
    outs.append(pltpu.make_async_copy(block, block_hbm, out_sems.at[0]))
    outs[2].start()
    next(temporal_sum)
    next(spatial_sum)
    outs.append(pltpu.make_async_copy(sums, sums_hbm, out_sems.at[3]))
    outs[3].start()
    for copy in outs:
        copy.wait()
    for copy in pending:
        copy.wait_send()


def finish_kernel(
    block_hbm, tgrad_hbm, sgrad_hbm, sums_hbm, o1, o2, o3, o4, o5, block, tgrad, sgrad, sums, s1, s2, in_sems, out_sems
):
    ins = [
        pltpu.make_async_copy(src, dst, in_sems.at[n])
        for n, (src, dst) in enumerate(
            ((sums_hbm, sums), (block_hbm, block), (tgrad_hbm, tgrad), (sgrad_hbm, sgrad))
        )
    ]
    for copy in ins:
        copy.start()
    ins[0].wait()
    for n, out in enumerate((s1, s2)):
        out[0:16] = sums[n, :, 0:72]
        out[16:18, 0:36] = sums[n, 0:2, 72:108]
        out[16:18, 36:72] = sums[n, 2:4, 72:108]
    outs = []
    for n, (src, dst) in enumerate(((s1, o4), (s2, o5), (block, o1), (tgrad, o2), (sgrad, o3))):
        if n >= 2:
            ins[n - 1].wait()
        outs.append(pltpu.make_async_copy(src, dst, out_sems.at[n]))
        outs[-1].start()
    for copy in outs:
        copy.wait()


def picker():
    pick = np.zeros((2, 4, 80, HD), np.float32)
    for zl in range(4):
        for x in range(4):
            for core in range(2):
                for i in range(18):
                    pick[core, x, zl * 18 + i, ((zl * 4 + x) * 2 + core) * 18 + i] = 1
    return jnp.asarray(pick.reshape(640, HD), BF)


def shards(tokens, spatial_qkv, wo_spatial, w_temporal, wo_temporal, cotangent):
    frames, patches, _ = tokens.shape
    sems = pltpu.SemaphoreType.DMA

    def vm(*shape, dtype=BF):
        return pltpu.VMEM(shape, dtype)

    scratch = [
        vm(ROWS, D), vm(ROWS, 3 * HD), vm(HD, D), vm(COLS, D), vm(D, 128), vm(HD, D), vm(ROWS, D),
        vm(640, HD), vm(4, 2, 4, 4, 144, 128),
        vm(ROWS, D), vm(8, 16, D), vm(8, 16, D), vm(8, 16, D), vm(8, 16, D),
        vm(8, 16, D), vm(8, 16, D), vm(8, 16, HD), vm(8, 16, HD),
        vm(8, ROWS, ROWS, dtype=F32), vm(8, ROWS, ROWS, dtype=F32),
        vm(ROWS, HD), vm(ROWS, 3 * HD), vm(16, ROWS, 128), vm(ROWS, HD), vm(ROWS, HD),
        vm(ROWS, 3 * HD), vm(ROWS, D), vm(ROWS, HD), vm(ROWS, 3 * HD), vm(ROWS, D),
        vm(8, 16, HD), vm(8, 16, HD), vm(8, 16, D), vm(8, 16, D),
        vm(2, 2, 320, ROWS), vm(2, 320, ROWS),
        vm(2, 4, 9, 80, 128), vm(2, 3, 9, 80, 128), vm(2, 4, 80, 384), vm(2, 3, 80, 384),
        vm(2, 16, 16, 128), vm(2, 15, 16, 128), vm(2, 16, 128, dtype=F32),
        sems((7,)), sems((4,)), sems,
        sems((4,)), sems((4,)), sems((4, 4)), sems((4, 4)), sems((4, 4)), sems((4, 4)),
        sems((4, 4)), sems((4, 4)), sems((5, 7)), sems((5, 7)), sems((4,)), sems((4,)),
        sems((2, 3)), sems((2, 3)), sems((2, 3)), sems((2, 3)), sems((2, 15)), sems((2, 15)),
    ]
    anywhere = pl.BlockSpec(memory_space=pl.ANY)
    block_out, tokens_grad, qkv_grad, sums = pl.pallas_call(
        kernel,
        out_shape=[
            jax.ShapeDtypeStruct((ROWS, D), BF), jax.ShapeDtypeStruct((ROWS, D), BF),
            jax.ShapeDtypeStruct((ROWS, 3 * HD), BF), jax.ShapeDtypeStruct((2, 16, 128), F32),
        ],
        in_specs=[anywhere] * 7,
        out_specs=[anywhere] * 4,
        scratch_shapes=scratch,
        compiler_params=pltpu.CompilerParams(
            collective_id=0, has_side_effects=True, vmem_limit_bytes=62 * 1024 * 1024
        ),
        name="block",
    )(
        tokens.reshape(ROWS, D), spatial_qkv.reshape(ROWS, 3 * HD), wo_spatial, w_temporal.T,
        wo_temporal, cotangent.reshape(ROWS, D), picker(),
    )
    block_out, tokens_grad, qkv_grad, spatial_sum, temporal_sum = pl.pallas_call(
        finish_kernel,
        out_shape=[
            jax.ShapeDtypeStruct((ROWS, D), BF), jax.ShapeDtypeStruct((ROWS, D), BF),
            jax.ShapeDtypeStruct((ROWS, 3 * HD), BF),
            jax.ShapeDtypeStruct((18, 72), F32), jax.ShapeDtypeStruct((18, 72), F32),
        ],
        in_specs=[anywhere] * 4,
        out_specs=[anywhere] * 5,
        scratch_shapes=[
            vm(ROWS, D), vm(ROWS, D), vm(ROWS, 3 * HD), vm(2, 16, 128, dtype=F32),
            vm(18, 72, dtype=F32), vm(18, 72, dtype=F32), sems((4,)), sems((5,)),
        ],
        name="finish",
    )(block_out, tokens_grad, qkv_grad, sums)
    return (
        block_out.reshape(frames, patches, D),
        tokens_grad.reshape(frames, patches, D),
        qkv_grad.reshape(frames, patches, 3 * HD),
        spatial_sum,
        temporal_sum,
    )


def solution(mesh):
    rows = P(("dp", "seq"), None, None)
    return jax.shard_map(
        shards,
        mesh=mesh,
        in_specs=(rows, rows, P(), P(None, "dp"), P(), rows),
        out_specs=(rows, rows, rows, P("seq", "dp"), P("seq", "dp")),
        check_vma=False,
    )
```
